256 devices in a mesh: row: 16 (over x_lo, z), col: 16 (over y, x_hi, core).
Axes of the slice: x: 4 (x_hi: 2, x_lo: 2; x = x_hi * 2 + x_lo), y: 4, z: 8, core: 2. Of those that a mesh axis runs over, the one named last changes fastest.
Arguments:
- x_first: bfloat16 [768, 18432], P(None, ('row', 'col')), may hold values from -1.5 to 1.5
- x_second: bfloat16 [768, 18432], P(None, ('row', 'col')), may hold values from -1.5 to 1.5
- w_first: bfloat16 [18432, 256], P(('row', 'col')), may hold values from -12 to 12
- w_second: bfloat16 [18432, 256], P(('row', 'col')), may hold values from -12 to 12
- counts: int32 [2], replicated, may hold values from 384 to 768
- damping: float32 [1], replicated, may hold values from 0.2 to 0.6
- eig_low: float32 [1], replicated, may hold values from 0.1 to 0.4
- eig_high: float32 [1], replicated, may hold values from 3 to 6
Outputs:
- merged: float32 [18432, 256], P(('row', 'col'))
- residual: float32 [18432, 256], P(('row', 'col'))
The draws below stay inside these ranges and needn't reach their ends.
Inputs may be any that keep to these rules, and one draw needn't show every extreme that they name: counts[i] is how many leading rows of domain i are used; later rows are ignored.
All inputs are finite; a program needn't handle non-finite values.
Results may differ from the reference program's by a relative error of at most 0.0003.
Values may be sent and summed in bfloat16 or wider, within the bound.
No kernel may reach another device: no remote copies, remote signals or barrier semaphores. Data moves between devices by JAX's collectives and lax.ppermute only.
A program may use at most 64 MiB of HBM per device.

```python
import jax
import jax.numpy as jnp
from jax import lax

D = 18432
ROWS = 768
COLS = 256
ITERS = 2


def shard_levels(own_key, shape, shards, smallest, high):
    level, own = 1.0, jax.random.fold_in(own_key, 6)
    for axis_at, blocks in shards:
        heights = jnp.exp(jax.random.uniform(jax.random.fold_in(own, axis_at), (blocks,), jnp.float32, smallest / len(shards), high / len(shards)))
        level = level * jnp.repeat(heights, shape[axis_at] // blocks).reshape([-1 if axis == axis_at else 1 for axis in range(len(shape))])
    return level


def bell_draw(stream_key, dims, deviation, reach, pieces=(), kind=jnp.bfloat16):
    result = jax.random.normal(stream_key, dims, jnp.float32) * deviation
    if len(pieces) > 0:
        result = shard_levels(stream_key, dims, pieces, -0.22, 0.18) * result
    return jnp.clip(result, min=-reach, max=reach).astype(kind)


def setup_inputs(seed: int = 0) -> dict:
    keys = jax.random.split(jax.random.key(seed), 9)
    x_first = bell_draw(keys[0], (ROWS, D), 0.25, 1.5, ((1, 256),))
    x_second = bell_draw(keys[1], (ROWS, D), 0.25, 1.5, ((1, 256),))
    w_first = bell_draw(keys[2], (D, COLS), 2.0, 12.0, ((0, 256),))
    w_second = bell_draw(keys[3], (D, COLS), 2.0, 12.0, ((0, 256),))
    counts = jax.random.randint(keys[4], (2,), ROWS // 2, ROWS + 1).astype(jnp.int32)
    damping = jnp.clip(jax.random.uniform(keys[5], (1,), jnp.float32, 0.2, 0.6), 0.2, 0.6)
    eig_low = jnp.clip(jax.random.uniform(keys[6], (1,), jnp.float32, 0.1, 0.4), 0.1, 0.4)
    eig_high = jnp.clip(jax.random.uniform(keys[7], (1,), jnp.float32, 3.0, 6.0), 3.0, 6.0)
    return {"x_first": x_first, "x_second": x_second, "w_first": w_first, "w_second": w_second, "counts": counts, "damping": damping, "eig_low": eig_low, "eig_high": eig_high}


def gram_apply(dense, scale, vector):
    inner = jnp.dot(dense, vector, precision=lax.Precision.HIGHEST, preferred_element_type=jnp.float32)
    return jnp.dot(dense.T, inner, precision=lax.Precision.HIGHEST, preferred_element_type=jnp.float32) * scale


def reference(x_first, x_second, w_first, w_second, counts, damping, eig_low, eig_high):
    position = jnp.arange(x_first.shape[0], dtype=jnp.int32)
    dense_first = x_first.astype(jnp.float32) * (position < counts[0]).astype(jnp.float32)[:, None]
    dense_second = x_second.astype(jnp.float32) * (position < counts[1]).astype(jnp.float32)[:, None]
    scale_first = 1.0 / counts[0].astype(jnp.float32)
    scale_second = 1.0 / counts[1].astype(jnp.float32)
    ridge = damping[0]
    rhs = gram_apply(dense_first, scale_first, w_first.astype(jnp.float32)) + gram_apply(dense_second, scale_second, w_second.astype(jnp.float32))
    middle = (eig_high[0] + eig_low[0]) / 2.0
    radius = (eig_high[0] - eig_low[0]) / 2.0
    sigma = middle / radius
    rho_now = 1.0 / sigma
    merged = jnp.zeros_like(rhs)
    residual = rhs
    direction = rhs / middle
    for step_index in range(ITERS):
        image = gram_apply(dense_first, scale_first, direction) + gram_apply(dense_second, scale_second, direction) + ridge * direction
        merged = merged + direction
        residual = residual - image
        rho_new = 1.0 / (2.0 * sigma - rho_now)
        direction = rho_new * rho_now * direction + (2.0 * rho_new / radius) * residual
        rho_now = rho_new
    return merged, residual
```

```python
import functools

import jax
import jax.numpy as jnp
from jax import lax
from jax.experimental import pallas as pl
from jax.experimental.pallas import tpu as pltpu
from jax.sharding import Mesh
from jax.sharding import PartitionSpec as P

AXES = ("xl", "z", "y", "xh", "core")
PLANE = ("xl", "y", "xh")
MEMBERS = ("xl", "y", "xh", "core")
NT = (((1,), (1,)), ((), ()))
NN = (((1,), (0,)), ((), ()))
VMEM = pl.BlockSpec(memory_space=pltpu.VMEM)
SMEM = pl.BlockSpec(memory_space=pltpu.SMEM)


def split_two(value):
    head = value.astype(jnp.bfloat16)
    tail = (value - head.astype(jnp.float32)).astype(jnp.bfloat16)
    return jnp.concatenate([head, tail], axis=0)


def times(value, feats, dims):
    out = lax.dot_general(split_two(value), feats, dims, preferred_element_type=jnp.float32)
    half = out.shape[0] // 2
    return out[:half] + out[half:]


def row_scale(counts_ref, rows):
    position = lax.broadcasted_iota(jnp.int32, (1, 2 * rows), 1)
    second = position >= rows
    within = jnp.where(second, position - rows, position)
    used = jnp.where(second, counts_ref[1], counts_ref[0])
    return jnp.where(within < used, 1.0 / used.astype(jnp.float32), 0.0)


def send_all(partial, out_ref):
    for k in range(out_ref.shape[0]):
        out_ref[k] = partial


def start_kernel(core_ref, w_ref, own_ref, other_ref, out_ref, held):
    core = core_ref[0]
    members = w_ref.shape[0] // 2
    width = w_ref.shape[2]
    rows = own_ref.shape[1] // 2
    total = None
    for half, feats in ((0, own_ref), (1, other_ref)):
        at = core if half == 0 else 1 - core
        for k in range(members):
            held[:, k * width : (k + 1) * width] = w_ref[2 * k + at].astype(jnp.float32)
        part = lax.dot_general(
            held[...].astype(jnp.bfloat16), feats[...], NN, preferred_element_type=jnp.float32
        )
        total = part if total is None else total + part
    cols = total.shape[0] // 2
    send_all(jnp.concatenate([total[:cols, :rows], total[cols:, rows:]], axis=1), out_ref)


def scalars(low_ref, high_ref):
    middle = (high_ref[0] + low_ref[0]) / 2.0
    radius = (high_ref[0] - low_ref[0]) / 2.0
    sigma = middle / radius
    rho = 1.0 / sigma
    rho_new = 1.0 / (2.0 * sigma - rho)
    return middle, radius, rho, rho_new


def back(parts_ref, counts_ref, feats):
    rows = parts_ref.shape[2] // 2
    inner = jnp.sum(parts_ref[...], axis=0) * row_scale(counts_ref, rows)
    return [times(inner, f[...], NT) for f in feats]


def ahead(direction, feats, out_ref):
    total = times(direction[0], feats[0][...], NN) + times(direction[1], feats[1][...], NN)
    send_all(total, out_ref)


def rhs_kernel(counts_ref, low_ref, high_ref, parts_ref, own_ref, other_ref, out_ref, rhs_ref):
    feats = (own_ref, other_ref)
    middle = scalars(low_ref, high_ref)[0]
    rhs = back(parts_ref, counts_ref, feats)
    for k in range(2):
        rhs_ref[k] = rhs[k]
    ahead([r / middle for r in rhs], feats, out_ref)


def step_kernel(
    counts_ref, low_ref, high_ref, ridge_ref, parts_ref, own_ref, other_ref, rhs_ref, out_ref, dir_ref, res_ref
):
    feats = (own_ref, other_ref)
    middle, radius, rho, rho_new = scalars(low_ref, high_ref)
    image = back(parts_ref, counts_ref, feats)
    direction = []
    for k in range(2):
        first = rhs_ref[k] / middle
        residual = rhs_ref[k] - (image[k] + ridge_ref[0] * first)
        direction.append(rho_new * rho * first + (2.0 * rho_new / radius) * residual)
        res_ref[k] = residual
        dir_ref[k] = direction[k]
    ahead(direction, feats, out_ref)


def last_kernel(
    core_ref,
    counts_ref,
    low_ref,
    high_ref,
    ridge_ref,
    parts_ref,
    own_ref,
    other_ref,
    rhs_ref,
    dir_ref,
    res_ref,
    out_ref,
    held,
):
    core = core_ref[0]
    feats = (own_ref, other_ref)
    middle = scalars(low_ref, high_ref)[0]
    image = back(parts_ref, counts_ref, feats)
    width = out_ref.shape[2]
    cols = rhs_ref.shape[1]
    members = out_ref.shape[0] // 2
    for half in range(2):
        at = core if half == 0 else 1 - core
        held[:cols] = rhs_ref[half] / middle + dir_ref[half]
        held[cols:] = res_ref[half] - (image[half] + ridge_ref[0] * dir_ref[half])
        for k in range(members):
            out_ref[2 * k + at] = held[:, k * width : (k + 1) * width]


def call(kernel, outs, specs, scratch=()):
    return pl.pallas_call(
        kernel,
        out_shape=outs,
        in_specs=specs,
        out_specs=jax.tree.map(lambda _: VMEM, outs),
        scratch_shapes=list(scratch),
        compiler_params=pltpu.CompilerParams(vmem_limit_bytes=40 * 1024 * 1024),
    )


def sum_parts(copies):
    return lax.all_to_all(copies, "z", 0, 0, tiled=True)


def body(x_first, x_second, w_first, w_second, counts, damping, eig_low, eig_high):
    f32 = jnp.float32
    rows, width = x_first.shape
    members = lax.axis_size(MEMBERS)
    plane = lax.axis_size(PLANE)
    depth = lax.axis_size("z")
    cols = w_first.shape[1] // members
    core = lax.axis_index("core").astype(jnp.int32).reshape(1)

    turned = jnp.concatenate([x_first.T, x_second.T], axis=1)
    w_turned = jnp.concatenate(
        [w_first.T.reshape(members, cols, width), w_second.T.reshape(members, cols, width)], axis=1
    )
    weights = lax.all_to_all(w_turned, MEMBERS, 0, 0, tiled=True)
    copies = jnp.broadcast_to(turned[None], (plane, width, 2 * rows))
    own = lax.all_to_all(copies, PLANE, 0, 0, tiled=True).reshape(plane * width, 2 * rows)
    other = lax.ppermute(own, "core", [(0, 1), (1, 0)])

    half = plane * width
    parts_shape = jax.ShapeDtypeStruct((depth, cols, 2 * rows), f32)
    state = jax.ShapeDtypeStruct((2, cols, half), f32)
    parts = call(
        start_kernel, parts_shape, [SMEM, VMEM, VMEM, VMEM], [pltpu.VMEM((2 * cols, half), f32)]
    )(core, weights, own, other)
    parts = sum_parts(parts)
    parts, rhs = call(rhs_kernel, (parts_shape, state), [SMEM] * 3 + [VMEM] * 3)(
        counts, eig_low, eig_high, parts, own, other
    )
    parts = sum_parts(parts)
    parts, direction, residual = call(
        step_kernel, (parts_shape, state, state), [SMEM] * 4 + [VMEM] * 4
    )(counts, eig_low, eig_high, damping, parts, own, other, rhs)
    parts = sum_parts(parts)
    out = call(
        last_kernel,
        jax.ShapeDtypeStruct((members, 2 * cols, width), f32),
        [SMEM] * 5 + [VMEM] * 6,
        [pltpu.VMEM((2 * cols, half), f32)],
    )(core, counts, eig_low, eig_high, damping, parts, own, other, rhs, direction, residual)
    out = lax.all_to_all(out, MEMBERS, 0, 0, tiled=True)
    merged = out[:, :cols].reshape(members * cols, width).T
    residual = out[:, cols:].reshape(members * cols, width).T
    return merged, residual


def solution(mesh):
    fine = Mesh(mesh.devices.reshape(2, 8, 4, 2, 2), AXES)
    return jax.shard_map(
        body,
        mesh=fine,
        in_specs=(
            P(None, AXES),
            P(None, AXES),
            P(AXES, None),
            P(AXES, None),
            P(),
            P(),
            P(),
            P(),
        ),
        out_specs=(P(AXES, None), P(AXES, None)),
        check_vma=False,
    )
```

```python
import jax
import jax.numpy as jnp
from jax import lax
from jax.experimental import pallas as pl
from jax.experimental.pallas import tpu as pltpu
from jax.sharding import Mesh
from jax.sharding import PartitionSpec as P

AXES = ("xl", "z", "y", "xh", "core")
MEMBERS = ("xl", "y", "xh", "core")
SIDE = 4
ORDER = (0, 1, 3, 2)
NT = (((1,), (1,)), ((), ()))
NN = (((1,), (0,)), ((), ()))
VMEM = pl.BlockSpec(memory_space=pltpu.VMEM)
SMEM = pl.BlockSpec(memory_space=pltpu.SMEM)


def member(x, y, core):
    return (((x % 2) * SIDE + y) * 2 + x // 2) * 2 + core


def ring_pairs(shift, first):
    pairs = []
    for x in range(SIDE):
        for y in range(SIDE):
            for core in range(2):
                if (core == 0) == first:
                    to = member(x, (y + shift) % SIDE, core)
                else:
                    to = member((x + shift) % SIDE, y, core)
                pairs.append((member(x, y, core), to))
    return pairs


def along(value, shift, first):
    return lax.ppermute(value, MEMBERS, ring_pairs(shift, first))


def swap(value):
    return lax.ppermute(value, "core", [(0, 1), (1, 0)])


def split_two(value):
    head = value.astype(jnp.bfloat16)
    tail = (value - head.astype(jnp.float32)).astype(jnp.bfloat16)
    return jnp.concatenate([head, tail], axis=0)


def times(value, feats, dims):
    out = lax.dot_general(split_two(value), feats, dims, preferred_element_type=jnp.float32)
    half = out.shape[0] // 2
    return out[:half] + out[half:]


def send_all(partial, out_ref):
    for k in range(out_ref.shape[0]):
        out_ref[k] = partial


def source(place_ref, first, second):
    x, y, core = place_ref[0], place_ref[1], place_ref[2]
    back_x = jnp.where(core == 0, second, first)
    back_y = jnp.where(core == 0, first, second)
    at_x = lax.rem(x + SIDE - back_x, SIDE)
    at_y = lax.rem(y + SIDE - back_y, SIDE)
    return ((lax.rem(at_x, 2) * SIDE + at_y) * 2 + lax.div(at_x, 2)) * 2


def piece(refs, outer, inner):
    deep = refs[0].shape[0] // SIDE
    if outer < 3:
        return refs[outer][inner * deep : (inner + 1) * deep]
    ref = refs[3 + inner // 2]
    return ref[(inner % 2) * deep : (inner % 2 + 1) * deep]


def start_kernel(place_ref, counts_ref, low_ref, high_ref, ridge_ref, w_ref, *refs):
    mine, theirs = refs[:5], refs[5:10]
    feats_ref, out_ref, scale_ref, coef_ref, held = refs[10:]
    core = place_ref[2]
    deep = mine[0].shape[0] // SIDE
    rows = mine[0].shape[1]
    width = deep // 2
    cols = w_ref.shape[2]
    for outer in range(SIDE):
        for inner in range(SIDE):
            at = (outer * SIDE + inner) * deep
            feats_ref[at : at + deep, :rows] = piece(mine, outer, inner)
            feats_ref[at : at + deep, rows:] = piece(theirs, inner, outer)
            origin = source(place_ref, ORDER[inner], ORDER[outer])
            for k in range(2):
                here = at + k * width
                held[:cols, here : here + width] = w_ref[origin + k, core].astype(jnp.float32)
                held[cols:, here : here + width] = w_ref[origin + k, 1 - core].astype(jnp.float32)
    weights = held[...].astype(jnp.bfloat16)
    first = lax.dot_general(
        weights[:cols], feats_ref[:, :rows], NN, preferred_element_type=jnp.float32
    )
    second = lax.dot_general(
        weights[cols:], feats_ref[:, rows:], NN, preferred_element_type=jnp.float32
    )
    send_all(jnp.concatenate([first, second], axis=1), out_ref)

    position = lax.broadcasted_iota(jnp.int32, (1, 2 * rows), 1)
    other = position >= rows
    within = jnp.where(other, position - rows, position)
    used = jnp.where(other, counts_ref[1 - core], counts_ref[core])
    scale_ref[...] = jnp.where(within < used, 1.0 / used.astype(jnp.float32), 0.0)

    one = jnp.ones((1, 128), jnp.float32)
    low, high = one * low_ref[0], one * high_ref[0]
    middle, radius = (high + low) / 2.0, (high - low) / 2.0
    sigma = middle / radius
    rho = 1.0 / sigma
    rho_new = 1.0 / (2.0 * sigma - rho)
    coef_ref[0:1] = middle
    coef_ref[1:2] = one * ridge_ref[0]
    coef_ref[2:3] = rho_new * rho
    coef_ref[3:4] = 2.0 * rho_new / radius


def ahead(direction, scale_ref, feats_ref, out_ref):
    feats = feats_ref[...]
    send_all(times(times(direction * scale_ref[...], feats, NT), feats, NN), out_ref)


def rhs_kernel(coef_ref, scale_ref, parts_ref, feats_ref, out_ref, rhs_ref):
    rhs = jnp.sum(parts_ref[...], axis=0)
    rhs_ref[...] = rhs
    ahead(rhs / coef_ref[0:1, 0:1], scale_ref, feats_ref, out_ref)


def step_kernel(coef_ref, scale_ref, parts_ref, feats_ref, rhs_ref, out_ref, dir_ref, res_ref):
    first = rhs_ref[...] / coef_ref[0:1, 0:1]
    image = jnp.sum(parts_ref[...], axis=0) + coef_ref[1:2, 0:1] * first
    residual = rhs_ref[...] - image
    direction = coef_ref[2:3, 0:1] * first + coef_ref[3:4, 0:1] * residual
    dir_ref[...] = direction
    res_ref[...] = residual
    ahead(direction, scale_ref, feats_ref, out_ref)


def last_kernel(
    place_ref, coef_ref, scale_ref, parts_ref, feats_ref, rhs_ref, dir_ref, res_ref, out_ref, held
):
    direction = dir_ref[...]
    image = jnp.sum(parts_ref[...], axis=0) + coef_ref[1:2, 0:1] * direction
    residual = res_ref[...] - image
    merged = rhs_ref[...] / coef_ref[0:1, 0:1] + direction
    both = jnp.concatenate([merged, residual], axis=0) * scale_ref[...]
    held[...] = times(both, feats_ref[...], NT)
    width = out_ref.shape[2]
    for outer in range(SIDE):
        for inner in range(SIDE):
            at = (outer * SIDE + inner) * 2 * width
            origin = source(place_ref, ORDER[inner], ORDER[outer])
            for k in range(2):
                out_ref[origin + k] = held[:, at + k * width : at + (k + 1) * width]


def call(kernel, outs, specs, scratch=()):
    return pl.pallas_call(
        kernel,
        out_shape=outs,
        in_specs=specs,
        out_specs=jax.tree.map(lambda _: VMEM, outs),
        scratch_shapes=list(scratch),
        compiler_params=pltpu.CompilerParams(vmem_limit_bytes=32 * 1024 * 1024),
    )


def sum_parts(copies):
    return lax.all_to_all(copies, "z", 0, 0, tiled=True)


def body(x_first, x_second, w_first, w_second, counts, damping, eig_low, eig_high):
    f32 = jnp.float32
    shape = jax.ShapeDtypeStruct
    rows, width = x_first.shape
    members = lax.axis_size(MEMBERS)
    depth = lax.axis_size("z")
    cols = w_first.shape[1] // members
    core = lax.axis_index("core")
    place = jnp.stack([lax.axis_index("xh") * 2 + lax.axis_index("xl"), lax.axis_index("y"), core])
    place = place.astype(jnp.int32)

    w_turned = jnp.stack(
        [w.T.reshape(members, cols, width) for w in (w_first, w_second)], axis=1
    )
    lead = core == 0
    mine = jnp.where(lead, x_first, x_second).T
    give = jnp.where(lead, x_second, x_first).T
    got = swap(give)
    block = jnp.where(
        lead, jnp.concatenate([mine, got], axis=0), jnp.concatenate([got, mine], axis=0)
    )
    near = jnp.concatenate([block] + [along(block, k, True) for k in ORDER[1:]], axis=0)
    near, w_turned = lax.optimization_barrier((near, w_turned))
    back, front = along(near, 1, False), along(near, 3, False)
    weights = lax.all_to_all(w_turned, MEMBERS, 0, 0, tiled=True)
    back, front, weights = lax.optimization_barrier((back, front, weights))
    half = near.shape[0] // 2
    far_low, far_high = along(back[:half], 1, False), along(front[half:], 3, False)
    pieces = [near, back, front, far_low, far_high]
    swapped = [swap(p) for p in pieces]


    total = members * width
    copies = shape((depth, cols, 2 * rows), f32)
    state = shape((cols, 2 * rows), f32)
    feats, parts, scale, coef = call(
        start_kernel,
        (
            shape((total, 2 * rows), jnp.bfloat16),
            copies,
            shape((1, 2 * rows), f32),
            shape((4, 128), f32),
        ),
        [SMEM] * 5 + [VMEM] * 11,
        [pltpu.VMEM((2 * cols, total), f32)],
    )(place, counts, eig_low, eig_high, damping, weights, *pieces, *swapped)
    parts = sum_parts(parts)
    parts, rhs = call(rhs_kernel, (copies, state), [VMEM] * 4)(coef, scale, parts, feats)
    parts = sum_parts(parts)
    parts, direction, residual = call(step_kernel, (copies, state, state), [VMEM] * 5)(
        coef, scale, parts, feats, rhs
    )
    parts = sum_parts(parts)
    out = call(
        last_kernel,
        shape((members, 2 * cols, width), f32),
        [SMEM] + [VMEM] * 7,
        [pltpu.VMEM((2 * cols, total), f32)],
    )(place, coef, scale, parts, feats, rhs, direction, residual)
    out = lax.all_to_all(out, MEMBERS, 0, 0, tiled=True)
    merged = out[:, :cols].reshape(members * cols, width).T
    residual = out[:, cols:].reshape(members * cols, width).T
    return merged, residual


def solution(mesh):
    fine = Mesh(mesh.devices.reshape(2, 8, SIDE, 2, 2), AXES)
    return jax.shard_map(
        body,
        mesh=fine,
        in_specs=(
            P(None, AXES),
            P(None, AXES),
            P(AXES, None),
            P(AXES, None),
            P(),
            P(),
            P(),
            P(),
        ),
        out_specs=(P(AXES, None), P(AXES, None)),
        check_vma=False,
    )
```

```python
import jax
import jax.numpy as jnp
from jax import lax
from jax.experimental import pallas as pl
from jax.experimental.pallas import tpu as pltpu
from jax.sharding import Mesh
from jax.sharding import PartitionSpec as P

AXES = ("xl", "z", "y", "xh", "core")
MEMBERS = ("xl", "y", "xh", "core")
SIDE = 4
ORDER = (0, 1, 3, 2)
TILE = 128
STEPS = 256.0
LARGEST = 32767.0
SMALLEST = 2.0**-125
NT = (((1,), (1,)), ((), ()))
NN = (((1,), (0,)), ((), ()))
VMEM = pl.BlockSpec(memory_space=pltpu.VMEM)
SMEM = pl.BlockSpec(memory_space=pltpu.SMEM)


def member(x, y, core):
    return (((x % 2) * SIDE + y) * 2 + x // 2) * 2 + core


def ring_pairs(shift, first):
    pairs = []
    for x in range(SIDE):
        for y in range(SIDE):
            for core in range(2):
                if (core == 0) == first:
                    to = member(x, (y + shift) % SIDE, core)
                else:
                    to = member((x + shift) % SIDE, y, core)
                pairs.append((member(x, y, core), to))
    return pairs


def along(value, shift, first):
    return lax.ppermute(value, MEMBERS, ring_pairs(shift, first))


def swap(value):
    return lax.ppermute(value, "core", [(0, 1), (1, 0)])


def split_two(value):
    head = value.astype(jnp.bfloat16)
    tail = (value - head.astype(jnp.float32)).astype(jnp.bfloat16)
    return jnp.concatenate([head, tail], axis=0)


def times(value, feats, dims):
    out = lax.dot_general(split_two(value), feats, dims, preferred_element_type=jnp.float32)
    half = out.shape[0] // 2
    return out[:half] + out[half:]


def code(value):
    rows, lanes = value.shape
    spot = lax.broadcasted_iota(jnp.int32, (rows, TILE), 1)
    notes = jnp.zeros((rows, TILE), jnp.float32)
    pieces = []
    for t in range(lanes // TILE):
        tile = value[:, t * TILE : (t + 1) * TILE]
        peak = jnp.maximum(jnp.max(jnp.abs(tile), axis=1, keepdims=True), SMALLEST)
        note = jnp.ceil(jnp.log2(peak) * STEPS) + 1.0
        pieces.append(jnp.round(tile * jnp.exp2(note * (-1.0 / STEPS)) * LARGEST))
        notes = jnp.where(spot == t, note, notes)
    return jnp.concatenate(pieces + [notes], axis=1).astype(jnp.int32).astype(jnp.int16)


def sum_coded(parts_ref, places):
    tiles = parts_ref.shape[2] // TILE - 1
    totals = [0.0] * tiles
    for place in places:
        part = parts_ref[place].astype(jnp.int32).astype(jnp.float32)
        scales = jnp.exp2(part[:, tiles * TILE :] * (1.0 / STEPS))
        for t in range(tiles):
            totals[t] = totals[t] + part[:, t * TILE : (t + 1) * TILE] * scales[:, t : t + 1]
    return jnp.concatenate(totals, axis=1) * (1.0 / LARGEST)


def send_all(partial, out_ref):
    coded = code(partial)
    for k in range(out_ref.shape[0]):
        out_ref[k] = coded


def source(place_ref, first, second):
    x, y, core = place_ref[0], place_ref[1], place_ref[2]
    back_x = jnp.where(core == 0, second, first)
    back_y = jnp.where(core == 0, first, second)
    at_x = lax.rem(x + SIDE - back_x, SIDE)
    at_y = lax.rem(y + SIDE - back_y, SIDE)
    return ((lax.rem(at_x, 2) * SIDE + at_y) * 2 + lax.div(at_x, 2)) * 2


def piece(refs, outer, inner):
    deep = refs[0].shape[0] // SIDE
    if outer < 3:
        return refs[outer][inner * deep : (inner + 1) * deep]
    ref = refs[3 + inner // 2]
    return ref[(inner % 2) * deep : (inner % 2 + 1) * deep]


def deal_kernel(place_ref, keep_ref, got_ref, *refs):
    out_refs, (held,) = refs[:SIDE], refs[SIDE:]
    lead = place_ref[2] == 0
    keep = keep_ref[...].astype(jnp.float32)
    got = got_ref[:, got_ref.shape[1] - keep.shape[1] :].astype(jnp.float32)
    chips, each = held.shape[1:3]
    for k, rows in enumerate((jnp.where(lead, keep, got), jnp.where(lead, got, keep))):
        turned = rows.T
        for chip in range(chips):
            held[k, chip] = turned[chip * each : (chip + 1) * each]
    line = jnp.where(lead, place_ref[1], place_ref[0])
    for k, out_ref in zip(ORDER, out_refs):
        at = lax.rem(line + k, SIDE)
        for across in range(SIDE):
            x, y = jnp.where(lead, across, at), jnp.where(lead, at, across)
            chip = (lax.rem(x, 2) * SIDE + y) * 2 + lax.div(x, 2)
            for core in range(2):
                rows = slice(across * each, (across + 1) * each)
                out_ref[core, rows] = held[core, chip].astype(out_ref.dtype)


def line_kernel(place_ref, near_ref, *refs):
    w_refs, out_refs, (held, total) = refs[:SIDE], refs[SIDE : 2 * SIDE], refs[2 * SIDE :]
    width = w_refs[0].shape[2]
    for j, w_ref in enumerate(w_refs):
        for k in range(2):
            at = (2 * j + k) * width
            held[:, at : at + width] = w_ref[k].astype(jnp.float32)
    out = lax.dot_general(
        held[...].astype(jnp.bfloat16), near_ref[...], NN, preferred_element_type=jnp.float32
    )
    each = out.shape[0] // SIDE
    for k in range(SIDE):
        total[k] = out[k * each : (k + 1) * each]
    across = jnp.where(place_ref[2] == 0, place_ref[0], place_ref[1])
    for k, out_ref in zip(ORDER, out_refs):
        out_ref[...] = total[lax.rem(across + k, SIDE)]


def plane_kernel(own_ref, back_ref, front_ref, far_ref, out_ref):
    total = own_ref[...] + back_ref[...] + front_ref[...] + far_ref[...]
    cols = out_ref.shape[1]
    coded = [code(total[k * cols : (k + 1) * cols]) for k in range(2)]
    for k in range(out_ref.shape[0]):
        out_ref[k] = coded[k % 2]


def rhs_kernel(place_ref, counts_ref, low_ref, high_ref, ridge_ref, parts_ref, *refs):
    mine, theirs = refs[:5], refs[5:10]
    feats_ref, out_ref, rhs_ref, scale_ref, coef_ref = refs[10:]
    core = place_ref[2]
    deep = mine[0].shape[0] // SIDE
    rows = mine[0].shape[1]
    for outer in range(SIDE):
        for inner in range(SIDE):
            at = (outer * SIDE + inner) * deep
            feats_ref[at : at + deep, :rows] = piece(mine, outer, inner)
            feats_ref[at : at + deep, rows:] = piece(theirs, inner, outer)

    position = lax.broadcasted_iota(jnp.int32, (1, 2 * rows), 1)
    other = position >= rows
    within = jnp.where(other, position - rows, position)
    used = jnp.where(other, counts_ref[1 - core], counts_ref[core])
    scale_ref[...] = jnp.where(within < used, 1.0 / used.astype(jnp.float32), 0.0)

    one = jnp.ones((1, 128), jnp.float32)
    low, high = one * low_ref[0], one * high_ref[0]
    middle, radius = (high + low) / 2.0, (high - low) / 2.0
    sigma = middle / radius
    rho = 1.0 / sigma
    rho_new = 1.0 / (2.0 * sigma - rho)
    coef_ref[0:1] = middle
    coef_ref[1:2] = one * ridge_ref[0]
    coef_ref[2:3] = rho_new * rho
    coef_ref[3:4] = 2.0 * rho_new / radius

    half = parts_ref.shape[0] // 2
    for at, side in ((core, 0), (1 - core, 1)):
        total = sum_coded(parts_ref, [2 * k + at for k in range(half)])
        rhs_ref[:, side * rows : (side + 1) * rows] = total
    ahead(rhs_ref[...] / coef_ref[0:1, 0:1], scale_ref, feats_ref, out_ref)


def ahead(direction, scale_ref, feats_ref, out_ref):
    feats = feats_ref[...]
    send_all(times(times(direction * scale_ref[...], feats, NT), feats, NN), out_ref)


def step_kernel(coef_ref, scale_ref, parts_ref, feats_ref, rhs_ref, out_ref, dir_ref, res_ref):
    first = rhs_ref[...] / coef_ref[0:1, 0:1]
    image = sum_coded(parts_ref, range(parts_ref.shape[0])) + coef_ref[1:2, 0:1] * first
    residual = rhs_ref[...] - image
    direction = coef_ref[2:3, 0:1] * first + coef_ref[3:4, 0:1] * residual
    dir_ref[...] = direction
    res_ref[...] = residual
    ahead(direction, scale_ref, feats_ref, out_ref)


def last_kernel(
    place_ref, coef_ref, scale_ref, parts_ref, feats_ref, rhs_ref, dir_ref, res_ref, out_ref, held
):
    direction = dir_ref[...]
    image = sum_coded(parts_ref, range(parts_ref.shape[0])) + coef_ref[1:2, 0:1] * direction
    residual = res_ref[...] - image
    merged = rhs_ref[...] / coef_ref[0:1, 0:1] + direction
    both = jnp.concatenate([merged, residual], axis=0) * scale_ref[...]
    held[...] = times(both, feats_ref[...], NT)
    width = out_ref.shape[2]
    for outer in range(SIDE):
        for inner in range(SIDE):
            at = (outer * SIDE + inner) * 2 * width
            origin = source(place_ref, ORDER[inner], ORDER[outer])
            for k in range(2):
                out_ref[origin + k] = held[:, at + k * width : at + (k + 1) * width]


def call(kernel, outs, specs, scratch=()):
    return pl.pallas_call(
        kernel,
        out_shape=outs,
        in_specs=specs,
        out_specs=jax.tree.map(lambda _: VMEM, outs),
        scratch_shapes=list(scratch),
        compiler_params=pltpu.CompilerParams(vmem_limit_bytes=32 * 1024 * 1024),
    )


def sum_parts(copies):
    return lax.all_to_all(copies, "z", 0, 0, tiled=True)


def body(x_first, x_second, w_first, w_second, counts, damping, eig_low, eig_high):
    f32 = jnp.float32
    shape = jax.ShapeDtypeStruct
    rows, width = x_first.shape
    members = lax.axis_size(MEMBERS)
    depth = lax.axis_size("z")
    cols = w_first.shape[1] // members
    core = lax.axis_index("core")
    place = jnp.stack([lax.axis_index("xh") * 2 + lax.axis_index("xl"), lax.axis_index("y"), core])
    place = place.astype(jnp.int32)

    lead = core == 0
    mine = jnp.where(lead, x_first, x_second).T
    give = jnp.where(lead, x_second, x_first).T
    keep_w, give_w = jnp.where(lead, w_first, w_second), jnp.where(lead, w_second, w_first)
    got_all = swap(jnp.concatenate([give, give_w], axis=1))
    got = got_all[:, :rows]
    block = jnp.where(
        lead, jnp.concatenate([mine, got], axis=0), jnp.concatenate([got, mine], axis=0)
    )
    ring = [along(block, k, True) for k in ORDER[1:]]

    hand = shape((2, SIDE * 2 * cols, width), jnp.bfloat16)
    dealt = call(
        deal_kernel,
        [hand] * SIDE,
        [SMEM] + [VMEM] * 2,
        [pltpu.VMEM((2, members // 2, 2 * cols, width), f32)],
    )(place, keep_w, got_all)
    dealt = [dealt[0]] + [along(d, k, True) for k, d in zip(ORDER[1:], dealt[1:])]
    ring, dealt = lax.optimization_barrier((ring, dealt))
    near = jnp.concatenate([block] + ring, axis=0)

    shares = call(
        line_kernel,
        [shape((2 * cols, rows), f32)] * SIDE,
        [SMEM] + [VMEM] * (1 + SIDE),
        [
            pltpu.VMEM((hand.shape[1], near.shape[0]), f32),
            pltpu.VMEM((SIDE, 2 * cols, rows), f32),
        ],
    )(place, near, *dealt)
    shares, ahead_near = lax.optimization_barrier((shares, near))
    shares = [shares[0]] + [along(d, k, False) for k, d in zip(ORDER[1:], shares[1:])]
    back, front = along(ahead_near, 1, False), along(ahead_near, 3, False)
    parts = call(plane_kernel, shape((2 * depth, cols, rows + TILE), jnp.int16), [VMEM] * SIDE)(*shares)
    half = near.shape[0] // 2
    far_low, far_high = along(back[:half], 1, False), along(front[half:], 3, False)
    parts = lax.all_to_all(parts, ("z", "core"), 0, 0, tiled=True)
    pieces = [near, back, front, far_low, far_high]
    swapped = [swap(p) for p in pieces]

    total = members * width
    copies = shape((depth, cols, 2 * rows + TILE), jnp.int16)
    state = shape((cols, 2 * rows), f32)
    feats, parts, rhs, scale, coef = call(
        rhs_kernel,
        (
            shape((total, 2 * rows), jnp.bfloat16),
            copies,
            state,
            shape((1, 2 * rows), f32),
            shape((4, 128), f32),
        ),
        [SMEM] * 5 + [VMEM] * 11,
    )(place, counts, eig_low, eig_high, damping, parts, *pieces, *swapped)
    parts = sum_parts(parts)
    parts, direction, residual = call(step_kernel, (copies, state, state), [VMEM] * 5)(
        coef, scale, parts, feats, rhs
    )
    parts = sum_parts(parts)
    out = call(
        last_kernel,
        shape((members, 2 * cols, width), f32),
        [SMEM] + [VMEM] * 7,
        [pltpu.VMEM((2 * cols, total), f32)],
    )(place, coef, scale, parts, feats, rhs, direction, residual)
    out = lax.all_to_all(out, MEMBERS, 0, 0, tiled=True)
    merged = out[:, :cols].reshape(members * cols, width).T
    residual = out[:, cols:].reshape(members * cols, width).T
    return merged, residual


def solution(mesh):
    fine = Mesh(mesh.devices.reshape(2, 8, SIDE, 2, 2), AXES)
    return jax.shard_map(
        body,
        mesh=fine,
        in_specs=(
            P(None, AXES),
            P(None, AXES),
            P(AXES, None),
            P(AXES, None),
            P(),
            P(),
            P(),
            P(),
        ),
        out_specs=(P(AXES, None), P(AXES, None)),
        check_vma=False,
    )
```

```python
import jax
import jax.numpy as jnp
from jax import lax
from jax.experimental import pallas as pl
from jax.experimental.pallas import tpu as pltpu
from jax.sharding import Mesh
from jax.sharding import PartitionSpec as P

AXES = ("xl", "z", "y", "xh", "core")
MEMBERS = ("xl", "y", "xh", "core")
SIDE = 4
ORDER = (0, 1, 3, 2)
TILE = 128
STEPS = 256.0
LARGEST = 32767.0
SMALLEST = 2.0**-125
NT = (((1,), (1,)), ((), ()))
NN = (((1,), (0,)), ((), ()))
VMEM = pl.BlockSpec(memory_space=pltpu.VMEM)
SMEM = pl.BlockSpec(memory_space=pltpu.SMEM)


def member(x, y, core):
    return (((x % 2) * SIDE + y) * 2 + x // 2) * 2 + core


def ring_pairs(shift):
    pairs = []
    for x in range(SIDE):
        for y in range(SIDE):
            for core in range(2):
                if core == 0:
                    to = member((x + shift) % SIDE, y, core)
                else:
                    to = member(x, (y + shift) % SIDE, core)
                pairs.append((member(x, y, core), to))
    return pairs


def lines(first):
    groups = []
    for core in range(2):
        for other in range(SIDE):
            spots = [(k, other) if (core == 0) != first else (other, k) for k in range(SIDE)]
            groups.append([member(x, y, core) for x, y in spots])
    return groups


def exchange(blocks, first):
    return lax.all_to_all(blocks, MEMBERS, 0, 0, axis_index_groups=lines(first), tiled=True)


def along(value, shift):
    return lax.ppermute(value, MEMBERS, ring_pairs(shift))


def swap(value):
    return lax.ppermute(value, "core", [(0, 1), (1, 0)])


def split_two(value):
    head = value.astype(jnp.bfloat16)
    tail = (value - head.astype(jnp.float32)).astype(jnp.bfloat16)
    return jnp.concatenate([head, tail], axis=0)


def times(value, feats, dims):
    out = lax.dot_general(split_two(value), feats, dims, preferred_element_type=jnp.float32)
    half = out.shape[0] // 2
    return out[:half] + out[half:]


def code(value):
    rows, lanes = value.shape
    spot = lax.broadcasted_iota(jnp.int32, (rows, TILE), 1)
    notes = jnp.zeros((rows, TILE), jnp.float32)
    pieces = []
    for t in range(lanes // TILE):
        tile = value[:, t * TILE : (t + 1) * TILE]
        peak = jnp.maximum(jnp.max(jnp.abs(tile), axis=1, keepdims=True), SMALLEST)
        note = jnp.ceil(jnp.log2(peak) * STEPS) + 1.0
        pieces.append(jnp.round(tile * jnp.exp2(note * (-1.0 / STEPS)) * LARGEST))
        notes = jnp.where(spot == t, note, notes)
    return jnp.concatenate(pieces + [notes], axis=1).astype(jnp.int32).astype(jnp.int16)


def sum_coded(parts_ref, places):
    tiles = parts_ref.shape[2] // TILE - 1
    totals = [0.0] * tiles
    for place in places:
        part = parts_ref[place].astype(jnp.int32).astype(jnp.float32)
        scales = jnp.exp2(part[:, tiles * TILE :] * (1.0 / STEPS))
        for t in range(tiles):
            totals[t] = totals[t] + part[:, t * TILE : (t + 1) * TILE] * scales[:, t : t + 1]
    return jnp.concatenate(totals, axis=1) * (1.0 / LARGEST)


def send_all(partial, out_ref):
    coded = code(partial)
    for k in range(out_ref.shape[0]):
        out_ref[k] = coded


def source(place_ref, first, second):
    x, y, core = place_ref[0], place_ref[1], place_ref[2]
    back_x = jnp.where(core == 0, second, first)
    back_y = jnp.where(core == 0, first, second)
    at_x = lax.rem(x + SIDE - back_x, SIDE)
    at_y = lax.rem(y + SIDE - back_y, SIDE)
    return ((lax.rem(at_x, 2) * SIDE + at_y) * 2 + lax.div(at_x, 2)) * 2


def line_place(place_ref):
    x, y, lead = place_ref[0], place_ref[1], place_ref[2] == 0
    return jnp.where(lead, y, x), jnp.where(lead, x, y)


def pack_kernel(place_ref, block_ref, keep_ref, got_ref, out_ref, held, strip):
    lead = place_ref[2] == 0
    deep = block_ref.shape[0]
    keep = keep_ref[...].astype(jnp.float32)
    got = got_ref[:, got_ref.shape[1] - keep.shape[1] :].astype(jnp.float32)
    chips, each, width = held.shape[1:]
    for k, rows in enumerate((jnp.where(lead, keep, got), jnp.where(lead, got, keep))):
        turned = rows.T
        for chip in range(chips):
            held[k, chip] = turned[chip * each : (chip + 1) * each]
    strip[...] = jnp.zeros_like(strip)
    for at in range(SIDE):
        out_ref[at, :deep] = block_ref[...]
        for across in range(SIDE):
            x, y = jnp.where(lead, across, at), jnp.where(lead, at, across)
            chip = (lax.rem(x, 2) * SIDE + y) * 2 + lax.div(x, 2)
            for core in range(2):
                here = (2 * across + core) * width
                strip[:, here : here + width] = held[core, chip]
        out_ref[at, deep:] = strip[...].astype(out_ref.dtype)


def line_kernel(packed_ref, near_ref, out_ref, held):
    places, deep, rows = near_ref.shape
    each = out_ref.shape[1]
    for at in range(places):
        strip = packed_ref[at, deep:].astype(jnp.float32)
        for across in range(SIDE):
            part = strip[:, across * deep : (across + 1) * deep]
            held[across * each : (across + 1) * each, at * deep : (at + 1) * deep] = part
    out = lax.dot_general(
        held[...].astype(jnp.bfloat16),
        near_ref[...].reshape(places * deep, rows),
        NN,
        preferred_element_type=jnp.float32,
    )
    for across in range(SIDE):
        out_ref[across] = out[across * each : (across + 1) * each]


def plane_kernel(shares_ref, out_ref):
    total = jnp.sum(shares_ref[...], axis=0)
    cols = out_ref.shape[1]
    coded = [code(total[k * cols : (k + 1) * cols]) for k in range(2)]
    for k in range(out_ref.shape[0]):
        out_ref[k] = coded[k % 2]


def rhs_kernel(place_ref, counts_ref, low_ref, high_ref, ridge_ref, parts_ref, *refs):
    mine, theirs = refs[:SIDE], refs[SIDE : 2 * SIDE]
    feats_ref, out_ref, rhs_ref, scale_ref, coef_ref = refs[2 * SIDE :]
    core = place_ref[2]
    deep, rows = mine[0].shape[1:]
    line, across = line_place(place_ref)
    for outer in range(SIDE):
        there = lax.rem(across + SIDE - ORDER[outer], SIDE)
        for inner in range(SIDE):
            here = lax.rem(line + SIDE - ORDER[inner], SIDE)
            at = (outer * SIDE + inner) * deep
            feats_ref[at : at + deep, :rows] = mine[outer][here]
            feats_ref[at : at + deep, rows:] = theirs[inner][there]

    position = lax.broadcasted_iota(jnp.int32, (1, 2 * rows), 1)
    other = position >= rows
    within = jnp.where(other, position - rows, position)
    used = jnp.where(other, counts_ref[1 - core], counts_ref[core])
    scale_ref[...] = jnp.where(within < used, 1.0 / used.astype(jnp.float32), 0.0)

    one = jnp.ones((1, 128), jnp.float32)
    low, high = one * low_ref[0], one * high_ref[0]
    middle, radius = (high + low) / 2.0, (high - low) / 2.0
    sigma = middle / radius
    rho = 1.0 / sigma
    rho_new = 1.0 / (2.0 * sigma - rho)
    coef_ref[0:1] = middle
    coef_ref[1:2] = one * ridge_ref[0]
    coef_ref[2:3] = rho_new * rho
    coef_ref[3:4] = 2.0 * rho_new / radius

    half = parts_ref.shape[0] // 2
    for at, side in ((core, 0), (1 - core, 1)):
        total = sum_coded(parts_ref, [2 * k + at for k in range(half)])
        rhs_ref[:, side * rows : (side + 1) * rows] = total
    ahead(rhs_ref[...] / coef_ref[0:1, 0:1], scale_ref, feats_ref, out_ref)


def ahead(direction, scale_ref, feats_ref, out_ref):
    feats = feats_ref[...]
    send_all(times(times(direction * scale_ref[...], feats, NT), feats, NN), out_ref)


def step_kernel(coef_ref, scale_ref, parts_ref, feats_ref, rhs_ref, out_ref, dir_ref, res_ref):
    first = rhs_ref[...] / coef_ref[0:1, 0:1]
    image = sum_coded(parts_ref, range(parts_ref.shape[0])) + coef_ref[1:2, 0:1] * first
    residual = rhs_ref[...] - image
    direction = coef_ref[2:3, 0:1] * first + coef_ref[3:4, 0:1] * residual
    dir_ref[...] = direction
    res_ref[...] = residual
    ahead(direction, scale_ref, feats_ref, out_ref)


def last_kernel(
    place_ref, coef_ref, scale_ref, parts_ref, feats_ref, rhs_ref, dir_ref, res_ref, out_ref, held
):
    direction = dir_ref[...]
    image = sum_coded(parts_ref, range(parts_ref.shape[0])) + coef_ref[1:2, 0:1] * direction
    residual = res_ref[...] - image
    merged = rhs_ref[...] / coef_ref[0:1, 0:1] + direction
    both = jnp.concatenate([merged, residual], axis=0) * scale_ref[...]
    held[...] = times(both, feats_ref[...], NT)
    width = out_ref.shape[2]
    for outer in range(SIDE):
        for inner in range(SIDE):
            at = (outer * SIDE + inner) * 2 * width
            origin = source(place_ref, ORDER[inner], ORDER[outer])
            for k in range(2):
                out_ref[origin + k] = held[:, at + k * width : at + (k + 1) * width]


def call(kernel, outs, specs, scratch=()):
    return pl.pallas_call(
        kernel,
        out_shape=outs,
        in_specs=specs,
        out_specs=jax.tree.map(lambda _: VMEM, outs),
        scratch_shapes=list(scratch),
        compiler_params=pltpu.CompilerParams(vmem_limit_bytes=32 * 1024 * 1024),
    )


def sum_parts(copies):
    return lax.all_to_all(copies, "z", 0, 0, tiled=True)


def body(x_first, x_second, w_first, w_second, counts, damping, eig_low, eig_high):
    f32 = jnp.float32
    shape = jax.ShapeDtypeStruct
    rows, width = x_first.shape
    members = lax.axis_size(MEMBERS)
    depth = lax.axis_size("z")
    cols = w_first.shape[1] // members
    core = lax.axis_index("core")
    place = jnp.stack([lax.axis_index("xh") * 2 + lax.axis_index("xl"), lax.axis_index("y"), core])
    place = place.astype(jnp.int32)

    lead = core == 0
    mine = jnp.where(lead, x_first, x_second).T
    give = jnp.where(lead, x_second, x_first).T
    keep_w, give_w = jnp.where(lead, w_first, w_second), jnp.where(lead, w_second, w_first)
    got_all = swap(jnp.concatenate([give, give_w], axis=1))
    got = got_all[:, :rows]
    block = jnp.where(
        lead, jnp.concatenate([mine, got], axis=0), jnp.concatenate([got, mine], axis=0)
    )
    packed = call(
        pack_kernel,
        shape((SIDE, block.shape[0] + 2 * cols, rows), jnp.bfloat16),
        [SMEM] + [VMEM] * 3,
        [pltpu.VMEM((2, members // 2, 2 * cols, width), f32), pltpu.VMEM((2 * cols, rows), f32)],
    )(place, block, keep_w, got_all)
    packed = exchange(packed, True)
    near = packed[:, : block.shape[0]]
    back, front = along(near, 1), along(near, 3)
    shares = call(
        line_kernel,
        shape((SIDE, 2 * cols, rows), f32),
        [VMEM] * 2,
        [pltpu.VMEM((SIDE * 2 * cols, SIDE * block.shape[0]), f32)],
    )(packed, near)
    shares = exchange(shares, False)
    shares, back, front = lax.optimization_barrier((shares, back, front))
    parts = call(plane_kernel, shape((2 * depth, cols, rows + TILE), jnp.int16), [VMEM])(shares)
    far = along(back, 1)
    parts = lax.all_to_all(parts, ("z", "core"), 0, 0, tiled=True)
    parts, far = lax.optimization_barrier((parts, far))
    pieces = [near, back, front, far]
    swapped = [swap(p) for p in pieces]

    total = members * width
    copies = shape((depth, cols, 2 * rows + TILE), jnp.int16)
    state = shape((cols, 2 * rows), f32)
    feats, parts, rhs, scale, coef = call(
        rhs_kernel,
        (
            shape((total, 2 * rows), jnp.bfloat16),
            copies,
            state,
            shape((1, 2 * rows), f32),
            shape((4, 128), f32),
        ),
        [SMEM] * 5 + [VMEM] * (1 + 2 * SIDE),
    )(place, counts, eig_low, eig_high, damping, parts, *pieces, *swapped)
    parts = sum_parts(parts)
    parts, direction, residual = call(step_kernel, (copies, state, state), [VMEM] * 5)(
        coef, scale, parts, feats, rhs
    )
    parts = sum_parts(parts)
    out = call(
        last_kernel,
        shape((members, 2 * cols, width), f32),
        [SMEM] + [VMEM] * 7,
        [pltpu.VMEM((2 * cols, total), f32)],
    )(place, coef, scale, parts, feats, rhs, direction, residual)
    out = lax.all_to_all(out, MEMBERS, 0, 0, tiled=True)
    merged = out[:, :cols].reshape(members * cols, width).T
    residual = out[:, cols:].reshape(members * cols, width).T
    return merged, residual


def solution(mesh):
    fine = Mesh(mesh.devices.reshape(2, 8, SIDE, 2, 2), AXES)
    return jax.shard_map(
        body,
        mesh=fine,
        in_specs=(
            P(None, AXES),
            P(None, AXES),
            P(AXES, None),
            P(AXES, None),
            P(),
            P(),
            P(),
            P(),
        ),
        out_specs=(P(AXES, None), P(AXES, None)),
        check_vma=False,
    )
```

```python
import jax
import jax.numpy as jnp
from jax import lax
from jax.experimental import pallas as pl
from jax.experimental.pallas import tpu as pltpu
from jax.sharding import Mesh
from jax.sharding import PartitionSpec as P

AXES = ("xl", "z", "y", "xh", "core")
MEMBERS = ("xl", "y", "xh", "core")
SIDE = 4
ORDER = (0, 1, 3, 2)
TILE = 128
STEPS = 256.0
LARGEST = 32767.0
SMALLEST = 2.0**-125
NT = (((1,), (1,)), ((), ()))
NN = (((1,), (0,)), ((), ()))
VMEM = pl.BlockSpec(memory_space=pltpu.VMEM)
SMEM = pl.BlockSpec(memory_space=pltpu.SMEM)


def member(x, y, core):
    return (((x % 2) * SIDE + y) * 2 + x // 2) * 2 + core


def ring_pairs(shift):
    pairs = []
    for x in range(SIDE):
        for y in range(SIDE):
            for core in range(2):
                if core == 0:
                    to = member((x + shift) % SIDE, y, core)
                else:
                    to = member(x, (y + shift) % SIDE, core)
                pairs.append((member(x, y, core), to))
    return pairs


def lines(first):
    groups = []
    for core in range(2):
        for other in range(SIDE):
            spots = [(k, other) if (core == 0) != first else (other, k) for k in range(SIDE)]
            groups.append([member(x, y, core) for x, y in spots])
    return groups


def exchange(blocks, first):
    return lax.all_to_all(blocks, MEMBERS, 0, 0, axis_index_groups=lines(first), tiled=True)


def along(value, shift):
    return lax.ppermute(value, MEMBERS, ring_pairs(shift))


def swap(value):
    return lax.ppermute(value, "core", [(0, 1), (1, 0)])


def split_two(value):
    head = value.astype(jnp.bfloat16)
    tail = (value - head.astype(jnp.float32)).astype(jnp.bfloat16)
    return jnp.concatenate([head, tail], axis=0)


def times(value, feats, dims):
    out = lax.dot_general(split_two(value), feats, dims, preferred_element_type=jnp.float32)
    half = out.shape[0] // 2
    return out[:half] + out[half:]


def code(value):
    rows, lanes = value.shape
    spot = lax.broadcasted_iota(jnp.int32, (rows, TILE), 1)
    notes = jnp.zeros((rows, TILE), jnp.float32)
    pieces = []
    for t in range(lanes // TILE):
        tile = value[:, t * TILE : (t + 1) * TILE]
        peak = jnp.maximum(jnp.max(jnp.abs(tile), axis=1, keepdims=True), SMALLEST)
        note = jnp.ceil(jnp.log2(peak) * STEPS) + 1.0
        pieces.append(jnp.round(tile * jnp.exp2(note * (-1.0 / STEPS)) * LARGEST))
        notes = jnp.where(spot == t, note, notes)
    return jnp.concatenate(pieces + [notes], axis=1).astype(jnp.int32).astype(jnp.int16)


def sum_coded(parts_ref, places):
    tiles = parts_ref.shape[2] // TILE - 1
    totals = [0.0] * tiles
    for place in places:
        part = parts_ref[place].astype(jnp.int32).astype(jnp.float32)
        scales = jnp.exp2(part[:, tiles * TILE :] * (1.0 / STEPS))
        for t in range(tiles):
            totals[t] = totals[t] + part[:, t * TILE : (t + 1) * TILE] * scales[:, t : t + 1]
    return jnp.concatenate(totals, axis=1) * (1.0 / LARGEST)


def send_all(partial, out_ref):
    coded = code(partial)
    for k in range(out_ref.shape[0]):
        out_ref[k] = coded


def source(place_ref, first, second):
    x, y, core = place_ref[0], place_ref[1], place_ref[2]
    back_x = jnp.where(core == 0, second, first)
    back_y = jnp.where(core == 0, first, second)
    at_x = lax.rem(x + SIDE - back_x, SIDE)
    at_y = lax.rem(y + SIDE - back_y, SIDE)
    return ((lax.rem(at_x, 2) * SIDE + at_y) * 2 + lax.div(at_x, 2)) * 2


def line_place(place_ref):
    x, y, lead = place_ref[0], place_ref[1], place_ref[2] == 0
    return jnp.where(lead, y, x), jnp.where(lead, x, y)


def pack_kernel(place_ref, block_ref, keep_ref, got_ref, out_ref, held, strip):
    lead = place_ref[2] == 0
    deep = block_ref.shape[0]
    keep = keep_ref[:, block_ref.shape[1] :].astype(jnp.float32)
    got = got_ref[:, block_ref.shape[1] :].astype(jnp.float32)
    chips, each, width = held.shape[1:]
    for k, rows in enumerate((jnp.where(lead, keep, got), jnp.where(lead, got, keep))):
        turned = rows.T
        for chip in range(chips):
            held[k, chip] = turned[chip * each : (chip + 1) * each]
    strip[...] = jnp.zeros_like(strip)
    for at in range(SIDE):
        out_ref[at, :deep] = block_ref[...]
        for across in range(SIDE):
            x, y = jnp.where(lead, across, at), jnp.where(lead, at, across)
            chip = (lax.rem(x, 2) * SIDE + y) * 2 + lax.div(x, 2)
            for core in range(2):
                here = (2 * across + core) * width
                strip[:, here : here + width] = held[core, chip]
        out_ref[at, deep:] = strip[...].astype(out_ref.dtype)


def line_kernel(packed_ref, near_ref, out_ref, held):
    places, deep, rows = near_ref.shape
    each = out_ref.shape[1]
    for at in range(places):
        strip = packed_ref[at, deep:].astype(jnp.float32)
        for across in range(SIDE):
            part = strip[:, across * deep : (across + 1) * deep]
            held[across * each : (across + 1) * each, at * deep : (at + 1) * deep] = part
    out = lax.dot_general(
        held[...].astype(jnp.bfloat16),
        near_ref[...].reshape(places * deep, rows),
        NN,
        preferred_element_type=jnp.float32,
    )
    for across in range(SIDE):
        out_ref[across] = out[across * each : (across + 1) * each]


def plane_kernel(shares_ref, out_ref):
    total = jnp.sum(shares_ref[...], axis=0)
    cols = out_ref.shape[1]
    coded = [code(total[k * cols : (k + 1) * cols]) for k in range(2)]
    for k in range(out_ref.shape[0]):
        out_ref[k] = coded[k % 2]


def lay_kernel(place_ref, *refs):
    mine, theirs = refs[:SIDE], refs[SIDE : SIDE + 2]
    own_ref, other_ref = refs[SIDE + 2 :]
    deep = mine[0].shape[1]
    line, _ = line_place(place_ref)
    for inner in range(SIDE):
        here = lax.rem(line + SIDE - ORDER[inner], SIDE)
        for outer in range(SIDE):
            at = (inner * SIDE + outer) * deep
            own_ref[at : at + deep] = mine[outer][here]
    lay_others(place_ref, theirs, other_ref)


def coef_kernel(place_ref, counts_ref, low_ref, high_ref, ridge_ref, scale_ref, coef_ref):
    core = place_ref[2]
    rows = scale_ref.shape[1] // 2
    position = lax.broadcasted_iota(jnp.int32, (1, 2 * rows), 1)
    other = position >= rows
    within = jnp.where(other, position - rows, position)
    used = jnp.where(other, counts_ref[1 - core], counts_ref[core])
    scale_ref[...] = jnp.where(within < used, 1.0 / used.astype(jnp.float32), 0.0)

    one = jnp.ones((1, 128), jnp.float32)
    low, high = one * low_ref[0], one * high_ref[0]
    middle, radius = (high + low) / 2.0, (high - low) / 2.0
    sigma = middle / radius
    rho = 1.0 / sigma
    rho_new = 1.0 / (2.0 * sigma - rho)
    coef_ref[0:1] = middle
    coef_ref[1:2] = one * ridge_ref[0]
    coef_ref[2:3] = rho_new * rho
    coef_ref[3:4] = 2.0 * rho_new / radius


def lay_others(place_ref, theirs, other_ref):
    deep = theirs[0].shape[1]
    _, across = line_place(place_ref)
    for inner in range(2):
        for outer in range(SIDE):
            there = lax.rem(across + SIDE - ORDER[outer], SIDE)
            at = (inner * SIDE + outer) * deep
            other_ref[at : at + deep] = theirs[inner][there]


def rhs_kernel(place_ref, coef_ref, scale_ref, parts_ref, own_ref, first_ref, *refs):
    theirs, (second_ref, out_ref, rhs_ref) = refs[:2], refs[2:]
    core = place_ref[2]
    rows = own_ref.shape[1]
    lay_others(place_ref, theirs, second_ref)
    half = parts_ref.shape[0] // 2
    for at, side in ((core, 0), (1 - core, 1)):
        total = sum_coded(parts_ref, [2 * k + at for k in range(half)])
        rhs_ref[:, side * rows : (side + 1) * rows] = total
    ahead(rhs_ref[...] / coef_ref[0:1, 0:1], scale_ref, (own_ref, first_ref, second_ref), out_ref)


def to_features(value, feats):
    own, first, second = (f[...] for f in feats)
    rows = own.shape[1]
    other = jnp.concatenate(
        [times(value[:, rows:], first, NT), times(value[:, rows:], second, NT)], axis=1
    )
    return times(value[:, :rows], own, NT) + other


def ahead(direction, scale_ref, feats, out_ref):
    own, first, second = (f[...] for f in feats)
    half = first.shape[0]
    inner = to_features(direction * scale_ref[...], feats)
    left = times(inner, own, NN)
    right = times(inner[:, :half], first, NN) + times(inner[:, half:], second, NN)
    send_all(jnp.concatenate([left, right], axis=1), out_ref)


def step_kernel(coef_ref, scale_ref, parts_ref, *refs):
    feats, (rhs_ref, out_ref, dir_ref, res_ref) = refs[:3], refs[3:]
    first = rhs_ref[...] / coef_ref[0:1, 0:1]
    image = sum_coded(parts_ref, range(parts_ref.shape[0])) + coef_ref[1:2, 0:1] * first
    residual = rhs_ref[...] - image
    direction = coef_ref[2:3, 0:1] * first + coef_ref[3:4, 0:1] * residual
    dir_ref[...] = direction
    res_ref[...] = residual
    ahead(direction, scale_ref, feats, out_ref)


def last_kernel(place_ref, coef_ref, scale_ref, parts_ref, *refs):
    feats, (rhs_ref, dir_ref, res_ref, out_ref, held) = refs[:3], refs[3:]
    direction = dir_ref[...]
    image = sum_coded(parts_ref, range(parts_ref.shape[0])) + coef_ref[1:2, 0:1] * direction
    residual = res_ref[...] - image
    merged = rhs_ref[...] / coef_ref[0:1, 0:1] + direction
    both = jnp.concatenate([merged, residual], axis=0) * scale_ref[...]
    held[...] = to_features(both, feats)
    width = out_ref.shape[2]
    for inner in range(SIDE):
        for outer in range(SIDE):
            at = (inner * SIDE + outer) * 2 * width
            origin = source(place_ref, ORDER[inner], ORDER[outer])
            for k in range(2):
                out_ref[origin + k] = held[:, at + k * width : at + (k + 1) * width]


def turn_kernel(blocks_ref, merged_ref, residual_ref):
    members, both, width = blocks_ref.shape
    cols = both // 2
    merged_ref[...] = blocks_ref[:, :cols].reshape(members * cols, width).T
    residual_ref[...] = blocks_ref[:, cols:].reshape(members * cols, width).T


def call(kernel, outs, specs, scratch=()):
    return pl.pallas_call(
        kernel,
        out_shape=outs,
        in_specs=specs,
        out_specs=jax.tree.map(lambda _: VMEM, outs),
        scratch_shapes=list(scratch),
        compiler_params=pltpu.CompilerParams(vmem_limit_bytes=32 * 1024 * 1024),
    )


def sum_parts(copies):
    return lax.all_to_all(copies, "z", 0, 0, tiled=True)


def body(x_first, x_second, w_first, w_second, counts, damping, eig_low, eig_high):
    f32 = jnp.float32
    shape = jax.ShapeDtypeStruct
    rows, width = x_first.shape
    members = lax.axis_size(MEMBERS)
    depth = lax.axis_size("z")
    cols = w_first.shape[1] // members
    core = lax.axis_index("core")
    place = jnp.stack([lax.axis_index("xh") * 2 + lax.axis_index("xl"), lax.axis_index("y"), core])
    place = place.astype(jnp.int32)

    lead = core == 0
    first = jnp.concatenate([x_first.T, w_first], axis=1)
    second = jnp.concatenate([x_second.T, w_second], axis=1)
    kept, give = jnp.where(lead, first, second), jnp.where(lead, second, first)
    got_all = swap(give)
    mine, got = kept[:, :rows], got_all[:, :rows]
    block = jnp.where(
        lead, jnp.concatenate([mine, got], axis=0), jnp.concatenate([got, mine], axis=0)
    )
    packed = call(
        pack_kernel,
        shape((SIDE, block.shape[0] + 2 * cols, rows), jnp.bfloat16),
        [SMEM] + [VMEM] * 3,
        [pltpu.VMEM((2, members // 2, 2 * cols, width), f32), pltpu.VMEM((2 * cols, rows), f32)],
    )(place, block, kept, got_all)
    packed = exchange(packed, True)
    near = packed[:, : block.shape[0]]
    back, front = along(near, 1), along(near, 3)
    shares = call(
        line_kernel,
        shape((SIDE, 2 * cols, rows), f32),
        [VMEM] * 2,
        [pltpu.VMEM((SIDE * 2 * cols, SIDE * block.shape[0]), f32)],
    )(packed, near)
    shares = exchange(shares, False)
    shares, back, front = lax.optimization_barrier((shares, back, front))
    parts = call(plane_kernel, shape((2 * depth, cols, rows + TILE), jnp.int16), [VMEM])(shares)
    far = along(back, 1)
    parts, eig_low, eig_high, damping = lax.optimization_barrier(
        (parts, eig_low, eig_high, damping)
    )
    scale, coef = call(
        coef_kernel, (shape((1, 2 * rows), f32), shape((4, 128), f32)), [SMEM] * 5
    )(place, counts, eig_low, eig_high, damping)
    parts = lax.all_to_all(parts, ("z", "core"), 0, 0, tiled=True)
    parts, far, scale, coef = lax.optimization_barrier((parts, far, scale, coef))
    pieces = [near, back, front, far]
    swapped = [swap(p) for p in pieces]

    total = members * width
    copies = shape((depth, cols, 2 * rows + TILE), jnp.int16)
    state = shape((cols, 2 * rows), f32)
    own, first = call(
        lay_kernel,
        (shape((total, rows), jnp.bfloat16), shape((total // 2, rows), jnp.bfloat16)),
        [SMEM] + [VMEM] * (SIDE + 2),
    )(place, *pieces, *swapped[:2])
    second, parts, rhs = call(
        rhs_kernel,
        (shape((total // 2, rows), jnp.bfloat16), copies, state),
        [SMEM] + [VMEM] * 7,
    )(place, coef, scale, parts, own, first, *swapped[2:])
    feats = (own, first, second)
    parts = sum_parts(parts)
    parts, direction, residual = call(step_kernel, (copies, state, state), [VMEM] * 7)(
        coef, scale, parts, *feats, rhs
    )
    parts = sum_parts(parts)
    out = call(
        last_kernel,
        shape((members, 2 * cols, width), f32),
        [SMEM] + [VMEM] * 9,
        [pltpu.VMEM((2 * cols, total), f32)],
    )(place, coef, scale, parts, *feats, rhs, direction, residual)
    out = lax.all_to_all(out, MEMBERS, 0, 0, tiled=True)
    turned = shape((width, members * cols), f32)
    return tuple(call(turn_kernel, (turned, turned), [VMEM])(out))


def solution(mesh):
    fine = Mesh(mesh.devices.reshape(2, 8, SIDE, 2, 2), AXES)
    return jax.shard_map(
        body,
        mesh=fine,
        in_specs=(
            P(None, AXES),
            P(None, AXES),
            P(AXES, None),
            P(AXES, None),
            P(),
            P(),
            P(),
            P(),
        ),
        out_specs=(P(AXES, None), P(AXES, None)),
        check_vma=False,
    )
```

```python
import jax
import jax.numpy as jnp
from jax import lax
from jax.experimental import pallas as pl
from jax.experimental.pallas import tpu as pltpu
from jax.sharding import Mesh
from jax.sharding import PartitionSpec as P

AXES = ("xl", "z", "y", "xh", "core")
MEMBERS = ("xl", "y", "xh", "core")
SIDE = 4
ORDER = (0, 1, 3, 2)
TILE = 128
STEPS = 256.0
LARGEST = 32767.0
SMALLEST = 2.0**-125
NT = (((1,), (1,)), ((), ()))
NN = (((1,), (0,)), ((), ()))
VMEM = pl.BlockSpec(memory_space=pltpu.VMEM)
SMEM = pl.BlockSpec(memory_space=pltpu.SMEM)


def member(x, y, core):
    return (((x % 2) * SIDE + y) * 2 + x // 2) * 2 + core


def ring_pairs(shift):
    pairs = []
    for x in range(SIDE):
        for y in range(SIDE):
            for core in range(2):
                if core == 0:
                    to = member((x + shift) % SIDE, y, core)
                else:
                    to = member(x, (y + shift) % SIDE, core)
                pairs.append((member(x, y, core), to))
    return pairs


def lines(first):
    groups = []
    for core in range(2):
        for other in range(SIDE):
            spots = [(k, other) if (core == 0) != first else (other, k) for k in range(SIDE)]
            groups.append([member(x, y, core) for x, y in spots])
    return groups


def exchange(blocks, first):
    return lax.all_to_all(blocks, MEMBERS, 0, 0, axis_index_groups=lines(first), tiled=True)


def along(value, shift):
    return lax.ppermute(value, MEMBERS, ring_pairs(shift))


def swap(value):
    return lax.ppermute(value, "core", [(0, 1), (1, 0)])


def split_two(value):
    head = value.astype(jnp.bfloat16)
    tail = (value - head.astype(jnp.float32)).astype(jnp.bfloat16)
    return jnp.concatenate([head, tail], axis=0)


def times(value, feats, dims):
    out = lax.dot_general(split_two(value), feats, dims, preferred_element_type=jnp.float32)
    half = out.shape[0] // 2
    return out[:half] + out[half:]


def code(value):
    rows, lanes = value.shape
    spot = lax.broadcasted_iota(jnp.int32, (rows, TILE), 1)
    notes = jnp.zeros((rows, TILE), jnp.float32)
    pieces = []
    for t in range(lanes // TILE):
        tile = value[:, t * TILE : (t + 1) * TILE]
        peak = jnp.maximum(jnp.max(jnp.abs(tile), axis=1, keepdims=True), SMALLEST)
        note = jnp.ceil(jnp.log2(peak) * STEPS) + 1.0
        pieces.append(jnp.round(tile * jnp.exp2(note * (-1.0 / STEPS)) * LARGEST))
        notes = jnp.where(spot == t, note, notes)
    return jnp.concatenate(pieces + [notes], axis=1).astype(jnp.int32).astype(jnp.int16)


def sum_coded(parts_ref, places):
    tiles = parts_ref.shape[2] // TILE - 1
    totals = [0.0] * tiles
    for place in places:
        part = parts_ref[place].astype(jnp.int32).astype(jnp.float32)
        scales = jnp.exp2(part[:, tiles * TILE :] * (1.0 / STEPS))
        for t in range(tiles):
            totals[t] = totals[t] + part[:, t * TILE : (t + 1) * TILE] * scales[:, t : t + 1]
    return jnp.concatenate(totals, axis=1) * (1.0 / LARGEST)


def send_all(partial, out_ref):
    coded = code(partial)
    for k in range(out_ref.shape[0]):
        out_ref[k] = coded


def source(place_ref, first, second):
    x, y, core = place_ref[0], place_ref[1], place_ref[2]
    back_x = jnp.where(core == 0, second, first)
    back_y = jnp.where(core == 0, first, second)
    at_x = lax.rem(x + SIDE - back_x, SIDE)
    at_y = lax.rem(y + SIDE - back_y, SIDE)
    return ((lax.rem(at_x, 2) * SIDE + at_y) * 2 + lax.div(at_x, 2)) * 2


def line_place(place_ref):
    x, y, lead = place_ref[0], place_ref[1], place_ref[2] == 0
    return jnp.where(lead, y, x), jnp.where(lead, x, y)


def pack_kernel(place_ref, block_ref, keep_ref, got_ref, out_ref, held, strip):
    lead = place_ref[2] == 0
    deep = block_ref.shape[0]
    keep = keep_ref[:, block_ref.shape[1] :].astype(jnp.float32)
    got = got_ref[:, block_ref.shape[1] :].astype(jnp.float32)
    chips, each, width = held.shape[1:]
    for k, rows in enumerate((jnp.where(lead, keep, got), jnp.where(lead, got, keep))):
        turned = rows.T
        for chip in range(chips):
            held[k, chip] = turned[chip * each : (chip + 1) * each]
    strip[...] = jnp.zeros_like(strip)
    for at in range(SIDE):
        out_ref[at, :deep] = block_ref[...]
        for across in range(SIDE):
            x, y = jnp.where(lead, across, at), jnp.where(lead, at, across)
            chip = (lax.rem(x, 2) * SIDE + y) * 2 + lax.div(x, 2)
            for core in range(2):
                here = (2 * across + core) * width
                strip[:, here : here + width] = held[core, chip]
        out_ref[at, deep:] = strip[...].astype(out_ref.dtype)


def line_kernel(packed_ref, near_ref, out_ref, held):
    places, deep, rows = near_ref.shape
    each = out_ref.shape[1]
    for at in range(places):
        strip = packed_ref[at, deep:].astype(jnp.float32)
        for across in range(SIDE):
            part = strip[:, across * deep : (across + 1) * deep]
            held[across * each : (across + 1) * each, at * deep : (at + 1) * deep] = part
    out = lax.dot_general(
        held[...].astype(jnp.bfloat16),
        near_ref[...].reshape(places * deep, rows),
        NN,
        preferred_element_type=jnp.float32,
    )
    for across in range(SIDE):
        out_ref[across] = out[across * each : (across + 1) * each]


def plane_kernel(shares_ref, _, out_ref, __):
    total = jnp.sum(shares_ref[...], axis=0)
    cols = out_ref.shape[1]
    coded = [code(total[k * cols : (k + 1) * cols]) for k in range(2)]
    for k in range(out_ref.shape[0]):
        out_ref[k] = coded[k % 2]


def lay_kernel(place_ref, *refs):
    mine, theirs = refs[:SIDE], refs[SIDE : SIDE + 2]
    own_ref, other_ref = refs[SIDE + 2 :]
    deep = mine[0].shape[1]
    line, _ = line_place(place_ref)
    for inner in range(SIDE):
        here = lax.rem(line + SIDE - ORDER[inner], SIDE)
        for outer in range(SIDE):
            at = (inner * SIDE + outer) * deep
            own_ref[at : at + deep] = mine[outer][here]
    lay_others(place_ref, theirs, other_ref)


def coef_kernel(place_ref, counts_ref, low_ref, high_ref, ridge_ref, scale_ref, coef_ref):
    core = place_ref[2]
    rows = scale_ref.shape[1] // 2
    position = lax.broadcasted_iota(jnp.int32, (1, 2 * rows), 1)
    other = position >= rows
    within = jnp.where(other, position - rows, position)
    used = jnp.where(other, counts_ref[1 - core], counts_ref[core])
    scale_ref[...] = jnp.where(within < used, 1.0 / used.astype(jnp.float32), 0.0)

    one = jnp.ones((1, 128), jnp.float32)
    low, high = one * low_ref[0], one * high_ref[0]
    middle, radius = (high + low) / 2.0, (high - low) / 2.0
    sigma = middle / radius
    rho = 1.0 / sigma
    rho_new = 1.0 / (2.0 * sigma - rho)
    coef_ref[0:1] = middle
    coef_ref[1:2] = one * ridge_ref[0]
    coef_ref[2:3] = rho_new * rho
    coef_ref[3:4] = 2.0 * rho_new / radius


def lay_others(place_ref, theirs, other_ref):
    deep = theirs[0].shape[1]
    _, across = line_place(place_ref)
    for inner in range(2):
        for outer in range(SIDE):
            there = lax.rem(across + SIDE - ORDER[outer], SIDE)
            at = (inner * SIDE + outer) * deep
            other_ref[at : at + deep] = theirs[inner][there]


def rhs_kernel(place_ref, coef_ref, scale_ref, parts_ref, own_ref, first_ref, *refs):
    theirs, (second_ref, out_ref, rhs_ref) = refs[:2], refs[2:]
    core = place_ref[2]
    rows = own_ref.shape[1]
    lay_others(place_ref, theirs, second_ref)
    half = parts_ref.shape[0] // 2
    for at, side in ((core, 0), (1 - core, 1)):
        total = sum_coded(parts_ref, [2 * k + at for k in range(half)])
        rhs_ref[:, side * rows : (side + 1) * rows] = total
    ahead(rhs_ref[...] / coef_ref[0:1, 0:1], scale_ref, (own_ref, first_ref, second_ref), out_ref)


def to_features(value, feats):
    own, first, second = (f[...] for f in feats)
    rows = own.shape[1]
    other = jnp.concatenate(
        [times(value[:, rows:], first, NT), times(value[:, rows:], second, NT)], axis=1
    )
    return times(value[:, :rows], own, NT) + other


def ahead(direction, scale_ref, feats, out_ref):
    own, first, second = (f[...] for f in feats)
    half = first.shape[0]
    inner = to_features(direction * scale_ref[...], feats)
    left = times(inner, own, NN)
    right = times(inner[:, :half], first, NN) + times(inner[:, half:], second, NN)
    send_all(jnp.concatenate([left, right], axis=1), out_ref)


def step_kernel(coef_ref, scale_ref, parts_ref, *refs):
    feats, (rhs_ref, out_ref, dir_ref, res_ref) = refs[:3], refs[3:]
    first = rhs_ref[...] / coef_ref[0:1, 0:1]
    image = sum_coded(parts_ref, range(parts_ref.shape[0])) + coef_ref[1:2, 0:1] * first
    residual = rhs_ref[...] - image
    direction = coef_ref[2:3, 0:1] * first + coef_ref[3:4, 0:1] * residual
    dir_ref[...] = direction
    res_ref[...] = residual
    ahead(direction, scale_ref, feats, out_ref)


def last_kernel(place_ref, coef_ref, scale_ref, parts_ref, *refs):
    feats, (rhs_ref, dir_ref, res_ref, out_ref, held) = refs[:3], refs[3:]
    direction = dir_ref[...]
    image = sum_coded(parts_ref, range(parts_ref.shape[0])) + coef_ref[1:2, 0:1] * direction
    residual = res_ref[...] - image
    merged = rhs_ref[...] / coef_ref[0:1, 0:1] + direction
    both = jnp.concatenate([merged, residual], axis=0) * scale_ref[...]
    held[...] = to_features(both, feats)
    width = out_ref.shape[2]
    for inner in range(SIDE):
        for outer in range(SIDE):
            at = (inner * SIDE + outer) * 2 * width
            origin = source(place_ref, ORDER[inner], ORDER[outer])
            for k in range(2):
                out_ref[origin + k] = held[:, at + k * width : at + (k + 1) * width]


def turn_kernel(blocks_ref, merged_ref, residual_ref):
    members, both, width = blocks_ref.shape
    cols = both // 2
    merged_ref[...] = blocks_ref[:, :cols].reshape(members * cols, width).T
    residual_ref[...] = blocks_ref[:, cols:].reshape(members * cols, width).T


def call(kernel, outs, specs, scratch=()):
    return pl.pallas_call(
        kernel,
        out_shape=outs,
        in_specs=specs,
        out_specs=jax.tree.map(lambda _: VMEM, outs),
        scratch_shapes=list(scratch),
        compiler_params=pltpu.CompilerParams(vmem_limit_bytes=32 * 1024 * 1024),
    )


def sum_parts(copies):
    return lax.all_to_all(copies, "z", 0, 0, tiled=True)


def body(x_first, x_second, w_first, w_second, counts, damping, eig_low, eig_high):
    f32 = jnp.float32
    shape = jax.ShapeDtypeStruct
    rows, width = x_first.shape
    members = lax.axis_size(MEMBERS)
    depth = lax.axis_size("z")
    cols = w_first.shape[1] // members
    core = lax.axis_index("core")
    place = jnp.stack([lax.axis_index("xh") * 2 + lax.axis_index("xl"), lax.axis_index("y"), core])
    place = place.astype(jnp.int32)

    lead = core == 0
    first = jnp.concatenate([x_first.T, w_first], axis=1)
    second = jnp.concatenate([x_second.T, w_second], axis=1)
    kept, give = jnp.where(lead, first, second), jnp.where(lead, second, first)
    got_all = swap(give)
    mine, got = kept[:, :rows], got_all[:, :rows]
    block = jnp.where(
        lead, jnp.concatenate([mine, got], axis=0), jnp.concatenate([got, mine], axis=0)
    )
    packed = call(
        pack_kernel,
        shape((SIDE, block.shape[0] + 2 * cols, rows), jnp.bfloat16),
        [SMEM] + [VMEM] * 3,
        [pltpu.VMEM((2, members // 2, 2 * cols, width), f32), pltpu.VMEM((2 * cols, rows), f32)],
    )(place, block, kept, got_all)
    packed = exchange(packed, True)
    near = packed[:, : block.shape[0]]
    back, front = along(near, 1), along(near, 3)
    shares = call(
        line_kernel,
        shape((SIDE, 2 * cols, rows), f32),
        [VMEM] * 2,
        [pltpu.VMEM((SIDE * 2 * cols, SIDE * block.shape[0]), f32)],
    )(packed, near)
    shares = exchange(shares, False)
    anywhere = pl.BlockSpec(memory_space=pl.ANY)
    parts, back = pl.pallas_call(
        plane_kernel,
        out_shape=(
            shape((2 * depth, cols, rows + TILE), jnp.int16),
            shape(back.shape, back.dtype),
        ),
        in_specs=[VMEM, anywhere],
        out_specs=(VMEM, anywhere),
        input_output_aliases={1: 1},
        compiler_params=pltpu.CompilerParams(vmem_limit_bytes=32 * 1024 * 1024),
    )(shares, back)
    far = along(back, 1)
    parts, eig_low, eig_high, damping = lax.optimization_barrier(
        (parts, eig_low, eig_high, damping)
    )
    scale, coef = call(
        coef_kernel, (shape((1, 2 * rows), f32), shape((4, 128), f32)), [SMEM] * 5
    )(place, counts, eig_low, eig_high, damping)
    parts = lax.all_to_all(parts, ("z", "core"), 0, 0, tiled=True)
    parts, far, scale, coef = lax.optimization_barrier((parts, far, scale, coef))
    pieces = [near, back, front, far]
    swapped = [swap(p) for p in pieces]

    total = members * width
    copies = shape((depth, cols, 2 * rows + TILE), jnp.int16)
    state = shape((cols, 2 * rows), f32)
    own, first = call(
        lay_kernel,
        (shape((total, rows), jnp.bfloat16), shape((total // 2, rows), jnp.bfloat16)),
        [SMEM] + [VMEM] * (SIDE + 2),
    )(place, *pieces, *swapped[:2])
    second, parts, rhs = call(
        rhs_kernel,
        (shape((total // 2, rows), jnp.bfloat16), copies, state),
        [SMEM] + [VMEM] * 7,
    )(place, coef, scale, parts, own, first, *swapped[2:])
    feats = (own, first, second)
    parts = sum_parts(parts)
    parts, direction, residual = call(step_kernel, (copies, state, state), [VMEM] * 7)(
        coef, scale, parts, *feats, rhs
    )
    parts = sum_parts(parts)
    out = call(
        last_kernel,
        shape((members, 2 * cols, width), f32),
        [SMEM] + [VMEM] * 9,
        [pltpu.VMEM((2 * cols, total), f32)],
    )(place, coef, scale, parts, *feats, rhs, direction, residual)
    out = lax.all_to_all(out, MEMBERS, 0, 0, tiled=True)
    turned = shape((width, members * cols), f32)
    return tuple(call(turn_kernel, (turned, turned), [VMEM])(out))


def solution(mesh):
    fine = Mesh(mesh.devices.reshape(2, 8, SIDE, 2, 2), AXES)
    return jax.shard_map(
        body,
        mesh=fine,
        in_specs=(
            P(None, AXES),
            P(None, AXES),
            P(AXES, None),
            P(AXES, None),
            P(),
            P(),
            P(),
            P(),
        ),
        out_specs=(P(AXES, None), P(AXES, None)),
        check_vma=False,
    )
```

```python
import jax
import jax.numpy as jnp
from jax import lax
from jax.experimental import pallas as pl
from jax.experimental.pallas import tpu as pltpu
from jax.sharding import Mesh
from jax.sharding import PartitionSpec as P

AXES = ("xl", "z", "y", "xh", "core")
MEMBERS = ("xl", "y", "xh", "core")
SIDE = 4
ORDER = (0, 1, 3, 2)
TILE = 128
STEPS = 256.0
LARGEST = 32767.0
SMALLEST = 2.0**-125
NT = (((1,), (1,)), ((), ()))
NN = (((1,), (0,)), ((), ()))
VMEM = pl.BlockSpec(memory_space=pltpu.VMEM)
SMEM = pl.BlockSpec(memory_space=pltpu.SMEM)


def member(x, y, core):
    return (((x % 2) * SIDE + y) * 2 + x // 2) * 2 + core


def ring_pairs(shift):
    pairs = []
    for x in range(SIDE):
        for y in range(SIDE):
            for core in range(2):
                if core == 0:
                    to = member((x + shift) % SIDE, y, core)
                else:
                    to = member(x, (y + shift) % SIDE, core)
                pairs.append((member(x, y, core), to))
    return pairs


def lines(first):
    groups = []
    for core in range(2):
        for other in range(SIDE):
            spots = [(k, other) if (core == 0) != first else (other, k) for k in range(SIDE)]
            groups.append([member(x, y, core) for x, y in spots])
    return groups


def exchange(blocks, first):
    return lax.all_to_all(blocks, MEMBERS, 0, 0, axis_index_groups=lines(first), tiled=True)


def along(value, shift):
    return lax.ppermute(value, MEMBERS, ring_pairs(shift))


def swap(value):
    return lax.ppermute(value, "core", [(0, 1), (1, 0)])


def split_two(value):
    head = value.astype(jnp.bfloat16)
    tail = (value - head.astype(jnp.float32)).astype(jnp.bfloat16)
    return jnp.concatenate([head, tail], axis=0)


def times(value, feats, dims):
    out = lax.dot_general(split_two(value), feats, dims, preferred_element_type=jnp.float32)
    half = out.shape[0] // 2
    return out[:half] + out[half:]


def code(value):
    rows, lanes = value.shape
    spot = lax.broadcasted_iota(jnp.int32, (rows, TILE), 1)
    notes = jnp.zeros((rows, TILE), jnp.float32)
    pieces = []
    for t in range(lanes // TILE):
        tile = value[:, t * TILE : (t + 1) * TILE]
        peak = jnp.maximum(jnp.max(jnp.abs(tile), axis=1, keepdims=True), SMALLEST)
        note = jnp.ceil(jnp.log2(peak) * STEPS) + 1.0
        pieces.append(jnp.round(tile * jnp.exp2(note * (-1.0 / STEPS)) * LARGEST))
        notes = jnp.where(spot == t, note, notes)
    return jnp.concatenate(pieces + [notes], axis=1).astype(jnp.int32).astype(jnp.int16)


def sum_coded(parts_ref, places):
    tiles = parts_ref.shape[2] // TILE - 1
    totals = [0.0] * tiles
    for place in places:
        part = parts_ref[place].astype(jnp.int32).astype(jnp.float32)
        scales = jnp.exp2(part[:, tiles * TILE :] * (1.0 / STEPS))
        for t in range(tiles):
            totals[t] = totals[t] + part[:, t * TILE : (t + 1) * TILE] * scales[:, t : t + 1]
    return jnp.concatenate(totals, axis=1) * (1.0 / LARGEST)


def send_all(partial, out_ref):
    coded = code(partial)
    for k in range(out_ref.shape[0]):
        out_ref[k] = coded


def source(place_ref, first, second):
    x, y, core = place_ref[0], place_ref[1], place_ref[2]
    back_x = jnp.where(core == 0, second, first)
    back_y = jnp.where(core == 0, first, second)
    at_x = lax.rem(x + SIDE - back_x, SIDE)
    at_y = lax.rem(y + SIDE - back_y, SIDE)
    return ((lax.rem(at_x, 2) * SIDE + at_y) * 2 + lax.div(at_x, 2)) * 2


def line_place(place_ref):
    x, y, lead = place_ref[0], place_ref[1], place_ref[2] == 0
    return jnp.where(lead, y, x), jnp.where(lead, x, y)


def pack_kernel(place_ref, block_ref, keep_ref, got_ref, out_ref, held, strip):
    lead = place_ref[2] == 0
    deep = block_ref.shape[0]
    keep = keep_ref[:, block_ref.shape[1] :].astype(jnp.float32)
    got = got_ref[:, block_ref.shape[1] :].astype(jnp.float32)
    chips, each, width = held.shape[1:]
    for k, rows in enumerate((jnp.where(lead, keep, got), jnp.where(lead, got, keep))):
        turned = rows.T
        for chip in range(chips):
            held[k, chip] = turned[chip * each : (chip + 1) * each]
    strip[...] = jnp.zeros_like(strip)
    for at in range(SIDE):
        out_ref[at, :deep] = block_ref[...]
        for across in range(SIDE):
            x, y = jnp.where(lead, across, at), jnp.where(lead, at, across)
            chip = (lax.rem(x, 2) * SIDE + y) * 2 + lax.div(x, 2)
            for core in range(2):
                here = (2 * across + core) * width
                strip[:, here : here + width] = held[core, chip]
        out_ref[at, deep:] = strip[...].astype(out_ref.dtype)


def line_kernel(packed_ref, near_ref, out_ref, held):
    places, deep, rows = near_ref.shape
    each = out_ref.shape[1]
    for at in range(places):
        strip = packed_ref[at, deep:].astype(jnp.float32)
        for across in range(SIDE):
            part = strip[:, across * deep : (across + 1) * deep]
            held[across * each : (across + 1) * each, at * deep : (at + 1) * deep] = part
    out = lax.dot_general(
        held[...].astype(jnp.bfloat16),
        near_ref[...].reshape(places * deep, rows),
        NN,
        preferred_element_type=jnp.float32,
    )
    for across in range(SIDE):
        out_ref[across] = out[across * each : (across + 1) * each]


def plane_kernel(shares_ref, _, out_ref, __):
    total = jnp.sum(shares_ref[...], axis=0)
    cols = out_ref.shape[1]
    coded = [code(total[k * cols : (k + 1) * cols]) for k in range(2)]
    for k in range(out_ref.shape[0]):
        out_ref[k] = coded[k % 2]


def lay_kernel(place_ref, near_ref, back_ref, other_ref, sems):
    deep = near_ref.shape[1]
    _, across = line_place(place_ref)
    copies = []
    for inner, source_ref in enumerate((near_ref, back_ref)):
        for outer in range(SIDE):
            there = lax.rem(across + SIDE - ORDER[outer], SIDE)
            spot = inner * SIDE + outer
            copies.append(
                pltpu.make_async_copy(
                    source_ref.at[there],
                    other_ref.at[pl.ds(spot * deep, deep)],
                    sems.at[spot],
                )
            )
    for copy in copies:
        copy.start()
    for copy in copies:
        copy.wait()


def coef_kernel(place_ref, counts_ref, low_ref, high_ref, ridge_ref, scale_ref, coef_ref):
    core = place_ref[2]
    rows = scale_ref.shape[1] // 2
    position = lax.broadcasted_iota(jnp.int32, (1, 2 * rows), 1)
    other = position >= rows
    within = jnp.where(other, position - rows, position)
    used = jnp.where(other, counts_ref[1 - core], counts_ref[core])
    scale_ref[...] = jnp.where(within < used, 1.0 / used.astype(jnp.float32), 0.0)

    one = jnp.ones((1, 128), jnp.float32)
    low, high = one * low_ref[0], one * high_ref[0]
    middle, radius = (high + low) / 2.0, (high - low) / 2.0
    sigma = middle / radius
    rho = 1.0 / sigma
    rho_new = 1.0 / (2.0 * sigma - rho)
    coef_ref[0:1] = middle
    coef_ref[1:2] = one * ridge_ref[0]
    coef_ref[2:3] = rho_new * rho
    coef_ref[3:4] = 2.0 * rho_new / radius


def lay_others(place_ref, theirs, other_ref):
    deep = theirs[0].shape[1]
    _, across = line_place(place_ref)
    for inner in range(2):
        for outer in range(SIDE):
            there = lax.rem(across + SIDE - ORDER[outer], SIDE)
            at = (inner * SIDE + outer) * deep
            other_ref[at : at + deep] = theirs[inner][there]


def rhs_kernel(place_ref, coef_ref, scale_ref, parts_ref, *refs):
    mine, (own_ref, rhs_ref, inner_ref) = refs[:SIDE], refs[SIDE:]
    core = place_ref[2]
    deep, rows = mine[0].shape[1:]
    line, _ = line_place(place_ref)
    for inner in range(SIDE):
        here = lax.rem(line + SIDE - ORDER[inner], SIDE)
        for outer in range(SIDE):
            at = (inner * SIDE + outer) * deep
            own_ref[at : at + deep] = mine[outer][here]
    half = parts_ref.shape[0] // 2
    for at, side in ((core, 0), (1 - core, 1)):
        total = sum_coded(parts_ref, [2 * k + at for k in range(half)])
        rhs_ref[:, side * rows : (side + 1) * rows] = total
    first = rhs_ref[:, :rows] / coef_ref[0:1, 0:1] * scale_ref[:, :rows]
    inner_ref[...] = times(first, own_ref[...], NT)


def first_kernel(place_ref, coef_ref, scale_ref, rhs_ref, inner_ref, own_ref, first_ref, *refs):
    theirs, (second_ref, out_ref) = refs[:2], refs[2:]
    lay_others(place_ref, theirs, second_ref)
    rows = own_ref.shape[1]
    feats = (own_ref, first_ref, second_ref)
    value = rhs_ref[:, rows:] / coef_ref[0:1, 0:1] * scale_ref[:, rows:]
    from_features(inner_ref[...] + others_to_features(value, feats), feats, out_ref)


def others_to_features(value, feats):
    return jnp.concatenate([times(value, f[...], NT) for f in feats[1:]], axis=1)


def to_features(value, feats):
    rows = feats[0].shape[1]
    own = times(value[:, :rows], feats[0][...], NT)
    return own + others_to_features(value[:, rows:], feats)


def from_features(inner, feats, out_ref):
    own, first, second = (f[...] for f in feats)
    half = first.shape[0]
    left = times(inner, own, NN)
    right = times(inner[:, :half], first, NN) + times(inner[:, half:], second, NN)
    send_all(jnp.concatenate([left, right], axis=1), out_ref)


def ahead(direction, scale_ref, feats, out_ref):
    from_features(to_features(direction * scale_ref[...], feats), feats, out_ref)


def step_kernel(coef_ref, scale_ref, parts_ref, *refs):
    feats, (rhs_ref, out_ref, dir_ref, res_ref) = refs[:3], refs[3:]
    first = rhs_ref[...] / coef_ref[0:1, 0:1]
    image = sum_coded(parts_ref, range(parts_ref.shape[0])) + coef_ref[1:2, 0:1] * first
    residual = rhs_ref[...] - image
    direction = coef_ref[2:3, 0:1] * first + coef_ref[3:4, 0:1] * residual
    dir_ref[...] = direction
    res_ref[...] = residual
    ahead(direction, scale_ref, feats, out_ref)


def last_kernel(place_ref, coef_ref, scale_ref, parts_ref, *refs):
    feats, (rhs_ref, dir_ref, res_ref, out_ref, held) = refs[:3], refs[3:]
    direction = dir_ref[...]
    image = sum_coded(parts_ref, range(parts_ref.shape[0])) + coef_ref[1:2, 0:1] * direction
    residual = res_ref[...] - image
    merged = rhs_ref[...] / coef_ref[0:1, 0:1] + direction
    both = jnp.concatenate([merged, residual], axis=0) * scale_ref[...]
    held[...] = to_features(both, feats)
    width = out_ref.shape[2]
    for inner in range(SIDE):
        for outer in range(SIDE):
            at = (inner * SIDE + outer) * 2 * width
            origin = source(place_ref, ORDER[inner], ORDER[outer])
            for k in range(2):
                out_ref[origin + k] = held[:, at + k * width : at + (k + 1) * width]


def turn_kernel(blocks_ref, merged_ref, residual_ref):
    members, both, width = blocks_ref.shape
    cols = both // 2
    merged_ref[...] = blocks_ref[:, :cols].reshape(members * cols, width).T
    residual_ref[...] = blocks_ref[:, cols:].reshape(members * cols, width).T


def call(kernel, outs, specs, scratch=()):
    return pl.pallas_call(
        kernel,
        out_shape=outs,
        in_specs=specs,
        out_specs=jax.tree.map(lambda _: VMEM, outs),
        scratch_shapes=list(scratch),
        compiler_params=pltpu.CompilerParams(vmem_limit_bytes=32 * 1024 * 1024),
    )


def sum_parts(copies):
    return lax.all_to_all(copies, "z", 0, 0, tiled=True)


def body(x_first, x_second, w_first, w_second, counts, damping, eig_low, eig_high):
    f32 = jnp.float32
    shape = jax.ShapeDtypeStruct
    rows, width = x_first.shape
    members = lax.axis_size(MEMBERS)
    depth = lax.axis_size("z")
    cols = w_first.shape[1] // members
    core = lax.axis_index("core")
    place = jnp.stack([lax.axis_index("xh") * 2 + lax.axis_index("xl"), lax.axis_index("y"), core])
    place = place.astype(jnp.int32)

    lead = core == 0
    first = jnp.concatenate([x_first.T, w_first], axis=1)
    second = jnp.concatenate([x_second.T, w_second], axis=1)
    kept, give = jnp.where(lead, first, second), jnp.where(lead, second, first)
    got_all = swap(give)
    mine, got = kept[:, :rows], got_all[:, :rows]
    block = jnp.where(
        lead, jnp.concatenate([mine, got], axis=0), jnp.concatenate([got, mine], axis=0)
    )
    packed = call(
        pack_kernel,
        shape((SIDE, block.shape[0] + 2 * cols, rows), jnp.bfloat16),
        [SMEM] + [VMEM] * 3,
        [pltpu.VMEM((2, members // 2, 2 * cols, width), f32), pltpu.VMEM((2 * cols, rows), f32)],
    )(place, block, kept, got_all)
    packed = exchange(packed, True)
    near = packed[:, : block.shape[0]]
    back, front = along(near, 1), along(near, 3)
    shares = call(
        line_kernel,
        shape((SIDE, 2 * cols, rows), f32),
        [VMEM] * 2,
        [pltpu.VMEM((SIDE * 2 * cols, SIDE * block.shape[0]), f32)],
    )(packed, near)
    shares = exchange(shares, False)
    anywhere = pl.BlockSpec(memory_space=pl.ANY)
    parts, back = pl.pallas_call(
        plane_kernel,
        out_shape=(
            shape((2 * depth, cols, rows + TILE), jnp.int16),
            shape(back.shape, back.dtype),
        ),
        in_specs=[VMEM, anywhere],
        out_specs=(VMEM, anywhere),
        input_output_aliases={1: 1},
        compiler_params=pltpu.CompilerParams(vmem_limit_bytes=32 * 1024 * 1024),
    )(shares, back)
    far = along(back, 1)
    parts, eig_low, eig_high, damping = lax.optimization_barrier(
        (parts, eig_low, eig_high, damping)
    )
    scale, coef = call(
        coef_kernel, (shape((1, 2 * rows), f32), shape((4, 128), f32)), [SMEM] * 5
    )(place, counts, eig_low, eig_high, damping)
    parts = lax.all_to_all(parts, ("z", "core"), 0, 0, tiled=True)
    total = members * width
    near_swapped, back_swapped = swap(near), swap(back)
    first = pl.pallas_call(
        lay_kernel,
        out_shape=shape((total // 2, rows), jnp.bfloat16),
        in_specs=[SMEM, anywhere, anywhere],
        out_specs=VMEM,
        scratch_shapes=[pltpu.SemaphoreType.DMA((2 * SIDE,))],
    )(place, near_swapped, back_swapped)
    parts, far, scale, coef, first = lax.optimization_barrier((parts, far, scale, coef, first))
    others = swap(front), swap(far)
    copies = shape((depth, cols, 2 * rows + TILE), jnp.int16)
    state = shape((cols, 2 * rows), f32)
    own, rhs, inner = call(
        rhs_kernel,
        (shape((total, rows), jnp.bfloat16), state, shape((cols, total), f32)),
        [SMEM] + [VMEM] * 7,
    )(place, coef, scale, parts, near, back, front, far)
    second, parts = call(
        first_kernel,
        (shape((total // 2, rows), jnp.bfloat16), copies),
        [SMEM] + [VMEM] * 8,
    )(place, coef, scale, rhs, inner, own, first, *others)
    feats = (own, first, second)
    parts = sum_parts(parts)
    parts, direction, residual = call(step_kernel, (copies, state, state), [VMEM] * 7)(
        coef, scale, parts, *feats, rhs
    )
    parts = sum_parts(parts)
    out = call(
        last_kernel,
        shape((members, 2 * cols, width), f32),
        [SMEM] + [VMEM] * 9,
        [pltpu.VMEM((2 * cols, total), f32)],
    )(place, coef, scale, parts, *feats, rhs, direction, residual)
    out = lax.all_to_all(out, MEMBERS, 0, 0, tiled=True)
    turned = shape((width, members * cols), f32)
    return tuple(call(turn_kernel, (turned, turned), [VMEM])(out))


def solution(mesh):
    fine = Mesh(mesh.devices.reshape(2, 8, SIDE, 2, 2), AXES)
    return jax.shard_map(
        body,
        mesh=fine,
        in_specs=(
            P(None, AXES),
            P(None, AXES),
            P(AXES, None),
            P(AXES, None),
            P(),
            P(),
            P(),
            P(),
        ),
        out_specs=(P(AXES, None), P(AXES, None)),
        check_vma=False,
    )
```

```python
import jax
import jax.numpy as jnp
from jax import lax
from jax.experimental import pallas as pl
from jax.experimental.pallas import tpu as pltpu
from jax.sharding import Mesh
from jax.sharding import PartitionSpec as P

AXES = ("xl", "z", "y", "xh", "core")
MEMBERS = ("xl", "y", "xh", "core")
SIDE = 4
ORDER = (0, 1, 3, 2)
TILE = 128
STEPS = 256.0
LARGEST = 32767.0
SMALLEST = 2.0**-125
NT = (((1,), (1,)), ((), ()))
NN = (((1,), (0,)), ((), ()))
VMEM = pl.BlockSpec(memory_space=pltpu.VMEM)
SMEM = pl.BlockSpec(memory_space=pltpu.SMEM)


def member(x, y, core):
    return (((x % 2) * SIDE + y) * 2 + x // 2) * 2 + core


def ring_pairs(shift):
    pairs = []
    for x in range(SIDE):
        for y in range(SIDE):
            for core in range(2):
                if core == 0:
                    to = member((x + shift) % SIDE, y, core)
                else:
                    to = member(x, (y + shift) % SIDE, core)
                pairs.append((member(x, y, core), to))
    return pairs


def lines(first):
    groups = []
    for core in range(2):
        for other in range(SIDE):
            spots = [(k, other) if (core == 0) != first else (other, k) for k in range(SIDE)]
            groups.append([member(x, y, core) for x, y in spots])
    return groups


def exchange(blocks, first):
    return lax.all_to_all(blocks, MEMBERS, 0, 0, axis_index_groups=lines(first), tiled=True)


def along(value, shift):
    return lax.ppermute(value, MEMBERS, ring_pairs(shift))


def swap(value):
    return lax.ppermute(value, "core", [(0, 1), (1, 0)])


def split_two(value):
    head = value.astype(jnp.bfloat16)
    tail = (value - head.astype(jnp.float32)).astype(jnp.bfloat16)
    return jnp.concatenate([head, tail], axis=0)


def times(value, feats, dims):
    out = lax.dot_general(split_two(value), feats, dims, preferred_element_type=jnp.float32)
    half = out.shape[0] // 2
    return out[:half] + out[half:]


def code(value):
    rows, lanes = value.shape
    spot = lax.broadcasted_iota(jnp.int32, (rows, TILE), 1)
    notes = jnp.zeros((rows, TILE), jnp.float32)
    pieces = []
    for t in range(lanes // TILE):
        tile = value[:, t * TILE : (t + 1) * TILE]
        peak = jnp.maximum(jnp.max(jnp.abs(tile), axis=1, keepdims=True), SMALLEST)
        note = jnp.ceil(jnp.log2(peak) * STEPS) + 1.0
        pieces.append(jnp.round(tile * jnp.exp2(note * (-1.0 / STEPS)) * LARGEST))
        notes = jnp.where(spot == t, note, notes)
    return jnp.concatenate(pieces + [notes], axis=1).astype(jnp.int32).astype(jnp.int16)


def sum_coded(parts_ref, places):
    tiles = parts_ref.shape[2] // TILE - 1
    totals = [0.0] * tiles
    for place in places:
        part = parts_ref[place].astype(jnp.int32).astype(jnp.float32)
        scales = jnp.exp2(part[:, tiles * TILE :] * (1.0 / STEPS))
        for t in range(tiles):
            totals[t] = totals[t] + part[:, t * TILE : (t + 1) * TILE] * scales[:, t : t + 1]
    return jnp.concatenate(totals, axis=1) * (1.0 / LARGEST)


def send_all(partial, out_ref):
    coded = code(partial)
    for k in range(out_ref.shape[0]):
        out_ref[k] = coded


def source(place_ref, first, second):
    x, y, core = place_ref[0], place_ref[1], place_ref[2]
    back_x = jnp.where(core == 0, second, first)
    back_y = jnp.where(core == 0, first, second)
    at_x = lax.rem(x + SIDE - back_x, SIDE)
    at_y = lax.rem(y + SIDE - back_y, SIDE)
    return ((lax.rem(at_x, 2) * SIDE + at_y) * 2 + lax.div(at_x, 2)) * 2


def line_place(place_ref):
    x, y, lead = place_ref[0], place_ref[1], place_ref[2] == 0
    return jnp.where(lead, y, x), jnp.where(lead, x, y)


def pack_kernel(place_ref, block_ref, keep_ref, got_ref, out_ref, held, strip):
    lead = place_ref[2] == 0
    deep = block_ref.shape[0]
    keep = keep_ref[:, block_ref.shape[1] :].astype(jnp.float32)
    got = got_ref[:, block_ref.shape[1] :].astype(jnp.float32)
    chips, each, width = held.shape[1:]
    for k, rows in enumerate((jnp.where(lead, keep, got), jnp.where(lead, got, keep))):
        turned = rows.T
        for chip in range(chips):
            held[k, chip] = turned[chip * each : (chip + 1) * each]
    strip[...] = jnp.zeros_like(strip)
    for at in range(SIDE):
        out_ref[at, :deep] = block_ref[...]
        for across in range(SIDE):
            x, y = jnp.where(lead, across, at), jnp.where(lead, at, across)
            chip = (lax.rem(x, 2) * SIDE + y) * 2 + lax.div(x, 2)
            for core in range(2):
                here = (2 * across + core) * width
                strip[:, here : here + width] = held[core, chip]
        out_ref[at, deep:] = strip[...].astype(out_ref.dtype)


def line_kernel(packed_ref, near_ref, out_ref, held):
    places, deep, rows = near_ref.shape
    each = out_ref.shape[1]
    for at in range(places):
        strip = packed_ref[at, deep:].astype(jnp.float32)
        for across in range(SIDE):
            part = strip[:, across * deep : (across + 1) * deep]
            held[across * each : (across + 1) * each, at * deep : (at + 1) * deep] = part
    out = lax.dot_general(
        held[...].astype(jnp.bfloat16),
        near_ref[...].reshape(places * deep, rows),
        NN,
        preferred_element_type=jnp.float32,
    )
    for across in range(SIDE):
        out_ref[across] = out[across * each : (across + 1) * each]


def plane_kernel(shares_ref, _, __, out_ref, *unused):
    total = jnp.sum(shares_ref[...], axis=0)
    cols = out_ref.shape[1]
    coded = [code(total[k * cols : (k + 1) * cols]) for k in range(2)]
    for k in range(out_ref.shape[0]):
        out_ref[k] = coded[k % 2]


def lay_kernel(place_ref, near_ref, back_ref, other_ref, sems):
    deep = near_ref.shape[1]
    _, across = line_place(place_ref)
    copies = []
    for inner, source_ref in enumerate((near_ref, back_ref)):
        for outer in range(SIDE):
            there = lax.rem(across + SIDE - ORDER[outer], SIDE)
            spot = inner * SIDE + outer
            copies.append(
                pltpu.make_async_copy(
                    source_ref.at[there],
                    other_ref.at[pl.ds(spot * deep, deep)],
                    sems.at[spot],
                )
            )
    for copy in copies:
        copy.start()
    for copy in copies:
        copy.wait()


def coef_kernel(place_ref, counts_ref, low_ref, high_ref, ridge_ref, scale_ref, coef_ref):
    core = place_ref[2]
    rows = scale_ref.shape[1] // 2
    position = lax.broadcasted_iota(jnp.int32, (1, 2 * rows), 1)
    other = position >= rows
    within = jnp.where(other, position - rows, position)
    used = jnp.where(other, counts_ref[1 - core], counts_ref[core])
    scale_ref[...] = jnp.where(within < used, 1.0 / used.astype(jnp.float32), 0.0)

    one = jnp.ones((1, 128), jnp.float32)
    low, high = one * low_ref[0], one * high_ref[0]
    middle, radius = (high + low) / 2.0, (high - low) / 2.0
    sigma = middle / radius
    rho = 1.0 / sigma
    rho_new = 1.0 / (2.0 * sigma - rho)
    coef_ref[0:1] = middle
    coef_ref[1:2] = one * ridge_ref[0]
    coef_ref[2:3] = rho_new * rho
    coef_ref[3:4] = 2.0 * rho_new / radius


def lay_others(place_ref, theirs, other_ref):
    deep = theirs[0].shape[1]
    _, across = line_place(place_ref)
    for inner in range(2):
        for outer in range(SIDE):
            there = lax.rem(across + SIDE - ORDER[outer], SIDE)
            at = (inner * SIDE + outer) * deep
            other_ref[at : at + deep] = theirs[inner][there]


def rhs_kernel(place_ref, coef_ref, scale_ref, parts_ref, *refs):
    mine, (own_ref, rhs_ref, inner_ref) = refs[:SIDE], refs[SIDE:]
    core = place_ref[2]
    deep, rows = mine[0].shape[1:]
    line, _ = line_place(place_ref)
    for inner in range(SIDE):
        here = lax.rem(line + SIDE - ORDER[inner], SIDE)
        for outer in range(SIDE):
            at = (inner * SIDE + outer) * deep
            own_ref[at : at + deep] = mine[outer][here]
    half = parts_ref.shape[0] // 2
    for at, side in ((core, 0), (1 - core, 1)):
        total = sum_coded(parts_ref, [2 * k + at for k in range(half)])
        rhs_ref[:, side * rows : (side + 1) * rows] = total
    first = rhs_ref[:, :rows] / coef_ref[0:1, 0:1] * scale_ref[:, :rows]
    inner_ref[...] = times(first, own_ref[...], NT)


def first_kernel(place_ref, coef_ref, scale_ref, rhs_ref, inner_ref, own_ref, first_ref, *refs):
    theirs, (second_ref, out_ref) = refs[:2], refs[2:]
    lay_others(place_ref, theirs, second_ref)
    rows = own_ref.shape[1]
    feats = (own_ref, first_ref, second_ref)
    value = rhs_ref[:, rows:] / coef_ref[0:1, 0:1] * scale_ref[:, rows:]
    from_features(inner_ref[...] + others_to_features(value, feats), feats, out_ref)


def others_to_features(value, feats):
    return jnp.concatenate([times(value, f[...], NT) for f in feats[1:]], axis=1)


def to_features(value, feats):
    rows = feats[0].shape[1]
    own = times(value[:, :rows], feats[0][...], NT)
    return own + others_to_features(value[:, rows:], feats)


def from_features(inner, feats, out_ref):
    own, first, second = (f[...] for f in feats)
    half = first.shape[0]
    left = times(inner, own, NN)
    right = times(inner[:, :half], first, NN) + times(inner[:, half:], second, NN)
    send_all(jnp.concatenate([left, right], axis=1), out_ref)


def ahead(direction, scale_ref, feats, out_ref):
    from_features(to_features(direction * scale_ref[...], feats), feats, out_ref)


def step_kernel(coef_ref, scale_ref, parts_ref, *refs):
    feats, (rhs_ref, out_ref, dir_ref, res_ref) = refs[:3], refs[3:]
    first = rhs_ref[...] / coef_ref[0:1, 0:1]
    image = sum_coded(parts_ref, range(parts_ref.shape[0])) + coef_ref[1:2, 0:1] * first
    residual = rhs_ref[...] - image
    direction = coef_ref[2:3, 0:1] * first + coef_ref[3:4, 0:1] * residual
    dir_ref[...] = direction
    res_ref[...] = residual
    ahead(direction, scale_ref, feats, out_ref)


def last_kernel(place_ref, coef_ref, scale_ref, parts_ref, *refs):
    feats, (rhs_ref, dir_ref, res_ref, out_ref, held) = refs[:3], refs[3:]
    direction = dir_ref[...]
    image = sum_coded(parts_ref, range(parts_ref.shape[0])) + coef_ref[1:2, 0:1] * direction
    residual = res_ref[...] - image
    merged = rhs_ref[...] / coef_ref[0:1, 0:1] + direction
    both = jnp.concatenate([merged, residual], axis=0) * scale_ref[...]
    held[...] = to_features(both, feats)
    width = out_ref.shape[2]
    for inner in range(SIDE):
        for outer in range(SIDE):
            at = (inner * SIDE + outer) * 2 * width
            origin = source(place_ref, ORDER[inner], ORDER[outer])
            for k in range(2):
                out_ref[origin + k] = held[:, at + k * width : at + (k + 1) * width]


def turn_kernel(blocks_ref, merged_ref, residual_ref):
    members, both, width = blocks_ref.shape
    cols = both // 2
    merged_ref[...] = blocks_ref[:, :cols].reshape(members * cols, width).T
    residual_ref[...] = blocks_ref[:, cols:].reshape(members * cols, width).T


def call(kernel, outs, specs, scratch=()):
    return pl.pallas_call(
        kernel,
        out_shape=outs,
        in_specs=specs,
        out_specs=jax.tree.map(lambda _: VMEM, outs),
        scratch_shapes=list(scratch),
        compiler_params=pltpu.CompilerParams(vmem_limit_bytes=32 * 1024 * 1024),
    )


def sum_parts(copies):
    return lax.all_to_all(copies, "z", 0, 0, tiled=True)


def body(x_first, x_second, w_first, w_second, counts, damping, eig_low, eig_high):
    f32 = jnp.float32
    shape = jax.ShapeDtypeStruct
    rows, width = x_first.shape
    members = lax.axis_size(MEMBERS)
    depth = lax.axis_size("z")
    cols = w_first.shape[1] // members
    core = lax.axis_index("core")
    place = jnp.stack([lax.axis_index("xh") * 2 + lax.axis_index("xl"), lax.axis_index("y"), core])
    place = place.astype(jnp.int32)

    lead = core == 0
    first = jnp.concatenate([x_first.T, w_first], axis=1)
    second = jnp.concatenate([x_second.T, w_second], axis=1)
    give = jnp.where(lead, second, first)
    give, *own_args = lax.optimization_barrier((give, x_first, x_second, w_first, w_second))
    kept = jnp.where(
        lead,
        jnp.concatenate([own_args[0].T, own_args[2]], axis=1),
        jnp.concatenate([own_args[1].T, own_args[3]], axis=1),
    )
    got_all = swap(give)
    mine, got = kept[:, :rows], got_all[:, :rows]
    block = jnp.where(
        lead, jnp.concatenate([mine, got], axis=0), jnp.concatenate([got, mine], axis=0)
    )
    packed = call(
        pack_kernel,
        shape((SIDE, block.shape[0] + 2 * cols, rows), jnp.bfloat16),
        [SMEM] + [VMEM] * 3,
        [pltpu.VMEM((2, members // 2, 2 * cols, width), f32), pltpu.VMEM((2 * cols, rows), f32)],
    )(place, block, kept, got_all)
    packed = exchange(packed, True)
    near = packed[:, : block.shape[0]]
    back, front = along(near, 1), along(near, 3)
    shares = call(
        line_kernel,
        shape((SIDE, 2 * cols, rows), f32),
        [VMEM] * 2,
        [pltpu.VMEM((SIDE * 2 * cols, SIDE * block.shape[0]), f32)],
    )(packed, near)
    shares, eig_low, eig_high, damping = lax.optimization_barrier(
        (shares, eig_low, eig_high, damping)
    )
    scale, coef = call(
        coef_kernel, (shape((1, 2 * rows), f32), shape((4, 128), f32)), [SMEM] * 5
    )(place, counts, eig_low, eig_high, damping)
    shares = exchange(shares, False)
    anywhere = pl.BlockSpec(memory_space=pl.ANY)
    parts, back = pl.pallas_call(
        plane_kernel,
        out_shape=(
            shape((2 * depth, cols, rows + TILE), jnp.int16),
            shape(back.shape, back.dtype),
        ),
        in_specs=[VMEM, anywhere, anywhere],
        out_specs=(VMEM, anywhere),
        input_output_aliases={1: 1},
        compiler_params=pltpu.CompilerParams(vmem_limit_bytes=32 * 1024 * 1024),
    )(shares, back, coef)
    far = along(back, 1)
    parts = lax.all_to_all(parts, ("z", "core"), 0, 0, tiled=True)
    total = members * width
    near_swapped, back_swapped = swap(near), swap(back)
    first = pl.pallas_call(
        lay_kernel,
        out_shape=shape((total // 2, rows), jnp.bfloat16),
        in_specs=[SMEM, anywhere, anywhere],
        out_specs=VMEM,
        scratch_shapes=[pltpu.SemaphoreType.DMA((2 * SIDE,))],
    )(place, near_swapped, back_swapped)
    parts, far, scale, coef, first = lax.optimization_barrier((parts, far, scale, coef, first))
    others = swap(front), swap(far)
    copies = shape((depth, cols, 2 * rows + TILE), jnp.int16)
    state = shape((cols, 2 * rows), f32)
    own, rhs, inner = call(
        rhs_kernel,
        (shape((total, rows), jnp.bfloat16), state, shape((cols, total), f32)),
        [SMEM] + [VMEM] * 7,
    )(place, coef, scale, parts, near, back, front, far)
    second, parts = call(
        first_kernel,
        (shape((total // 2, rows), jnp.bfloat16), copies),
        [SMEM] + [VMEM] * 8,
    )(place, coef, scale, rhs, inner, own, first, *others)
    feats = (own, first, second)
    parts = sum_parts(parts)
    parts, direction, residual = call(step_kernel, (copies, state, state), [VMEM] * 7)(
        coef, scale, parts, *feats, rhs
    )
    parts = sum_parts(parts)
    out = call(
        last_kernel,
        shape((members, 2 * cols, width), f32),
        [SMEM] + [VMEM] * 9,
        [pltpu.VMEM((2 * cols, total), f32)],
    )(place, coef, scale, parts, *feats, rhs, direction, residual)
    out = lax.all_to_all(out, MEMBERS, 0, 0, tiled=True)
    turned = shape((width, members * cols), f32)
    return tuple(call(turn_kernel, (turned, turned), [VMEM])(out))


def solution(mesh):
    fine = Mesh(mesh.devices.reshape(2, 8, SIDE, 2, 2), AXES)
    return jax.shard_map(
        body,
        mesh=fine,
        in_specs=(
            P(None, AXES),
            P(None, AXES),
            P(AXES, None),
            P(AXES, None),
            P(),
            P(),
            P(),
            P(),
        ),
        out_specs=(P(AXES, None), P(AXES, None)),
        check_vma=False,
    )
```

```python
import jax
import jax.numpy as jnp
from jax import lax
from jax.experimental import pallas as pl
from jax.experimental.pallas import tpu as pltpu
from jax.sharding import Mesh
from jax.sharding import PartitionSpec as P

AXES = ("xl", "z", "y", "xh", "core")
MEMBERS = ("xl", "y", "xh", "core")
SIDE = 4
ORDER = (0, 1, 3, 2)
TILE = 128
STEPS = 256.0
LARGEST = 32767.0
SMALLEST = 2.0**-125
NT = (((1,), (1,)), ((), ()))
NN = (((1,), (0,)), ((), ()))
VMEM = pl.BlockSpec(memory_space=pltpu.VMEM)
SMEM = pl.BlockSpec(memory_space=pltpu.SMEM)


def member(x, y, core):
    return (((x % 2) * SIDE + y) * 2 + x // 2) * 2 + core


def ring_pairs(shift):
    pairs = []
    for x in range(SIDE):
        for y in range(SIDE):
            for core in range(2):
                if core == 0:
                    to = member((x + shift) % SIDE, y, core)
                else:
                    to = member(x, (y + shift) % SIDE, core)
                pairs.append((member(x, y, core), to))
    return pairs


def lines(first):
    groups = []
    for core in range(2):
        for other in range(SIDE):
            spots = [(k, other) if (core == 0) != first else (other, k) for k in range(SIDE)]
            groups.append([member(x, y, core) for x, y in spots])
    return groups


def exchange(blocks, first):
    return lax.all_to_all(blocks, MEMBERS, 0, 0, axis_index_groups=lines(first), tiled=True)


def along(value, shift):
    return lax.ppermute(value, MEMBERS, ring_pairs(shift))


def swap(value):
    return lax.ppermute(value, "core", [(0, 1), (1, 0)])


def split_two(value):
    head = value.astype(jnp.bfloat16)
    tail = (value - head.astype(jnp.float32)).astype(jnp.bfloat16)
    return jnp.concatenate([head, tail], axis=0)


def times(value, feats, dims):
    out = lax.dot_general(split_two(value), feats, dims, preferred_element_type=jnp.float32)
    half = out.shape[0] // 2
    return out[:half] + out[half:]


def code(value):
    rows, lanes = value.shape
    spot = lax.broadcasted_iota(jnp.int32, (rows, TILE), 1)
    notes = jnp.zeros((rows, TILE), jnp.float32)
    pieces = []
    for t in range(lanes // TILE):
        tile = value[:, t * TILE : (t + 1) * TILE]
        peak = jnp.maximum(jnp.max(jnp.abs(tile), axis=1, keepdims=True), SMALLEST)
        note = jnp.ceil(jnp.log2(peak) * STEPS) + 1.0
        pieces.append(jnp.round(tile * jnp.exp2(note * (-1.0 / STEPS)) * LARGEST))
        notes = jnp.where(spot == t, note, notes)
    return jnp.concatenate(pieces + [notes], axis=1).astype(jnp.int32).astype(jnp.int16)


def sum_coded(parts_ref, places):
    tiles = parts_ref.shape[2] // TILE - 1
    totals = [0.0] * tiles
    for place in places:
        part = parts_ref[place].astype(jnp.int32).astype(jnp.float32)
        scales = jnp.exp2(part[:, tiles * TILE :] * (1.0 / STEPS))
        for t in range(tiles):
            totals[t] = totals[t] + part[:, t * TILE : (t + 1) * TILE] * scales[:, t : t + 1]
    return jnp.concatenate(totals, axis=1) * (1.0 / LARGEST)


def send_all(partial, out_ref):
    coded = code(partial)
    for k in range(out_ref.shape[0]):
        out_ref[k] = coded


def source(place_ref, first, second):
    x, y, core = place_ref[0], place_ref[1], place_ref[2]
    back_x = jnp.where(core == 0, second, first)
    back_y = jnp.where(core == 0, first, second)
    at_x = lax.rem(x + SIDE - back_x, SIDE)
    at_y = lax.rem(y + SIDE - back_y, SIDE)
    return ((lax.rem(at_x, 2) * SIDE + at_y) * 2 + lax.div(at_x, 2)) * 2


def line_place(place_ref):
    x, y, lead = place_ref[0], place_ref[1], place_ref[2] == 0
    return jnp.where(lead, y, x), jnp.where(lead, x, y)


def pack_kernel(place_ref, block_ref, keep_ref, got_ref, out_ref, held, strip):
    lead = place_ref[2] == 0
    deep = block_ref.shape[0]
    keep = keep_ref[:, block_ref.shape[1] :].astype(jnp.float32)
    got = got_ref[:, block_ref.shape[1] :].astype(jnp.float32)
    chips, each, width = held.shape[1:]
    for k, rows in enumerate((jnp.where(lead, keep, got), jnp.where(lead, got, keep))):
        turned = rows.T
        for chip in range(chips):
            held[k, chip] = turned[chip * each : (chip + 1) * each]
    strip[...] = jnp.zeros_like(strip)
    for at in range(SIDE):
        out_ref[at, :deep] = block_ref[...]
        for across in range(SIDE):
            x, y = jnp.where(lead, across, at), jnp.where(lead, at, across)
            chip = (lax.rem(x, 2) * SIDE + y) * 2 + lax.div(x, 2)
            for core in range(2):
                here = (2 * across + core) * width
                strip[:, here : here + width] = held[core, chip]
        out_ref[at, deep:] = strip[...].astype(out_ref.dtype)


def line_kernel(packed_ref, near_ref, out_ref, held):
    places, deep, rows = near_ref.shape
    each = out_ref.shape[1]
    for at in range(places):
        strip = packed_ref[at, deep:].astype(jnp.float32)
        for across in range(SIDE):
            part = strip[:, across * deep : (across + 1) * deep]
            held[across * each : (across + 1) * each, at * deep : (at + 1) * deep] = part
    out = lax.dot_general(
        held[...].astype(jnp.bfloat16),
        near_ref[...].reshape(places * deep, rows),
        NN,
        preferred_element_type=jnp.float32,
    )
    for across in range(SIDE):
        out_ref[across] = code(out[across * each : (across + 1) * each])


def plane_kernel(shares_ref, _, __, out_ref, *unused):
    total = sum_coded(shares_ref, range(shares_ref.shape[0]))
    cols = out_ref.shape[1]
    coded = [code(total[k * cols : (k + 1) * cols]) for k in range(2)]
    for k in range(out_ref.shape[0]):
        out_ref[k] = coded[k % 2]


def lay_kernel(place_ref, near_ref, back_ref, other_ref, sems):
    deep = near_ref.shape[1]
    _, across = line_place(place_ref)
    copies = []
    for inner, source_ref in enumerate((near_ref, back_ref)):
        for outer in range(SIDE):
            there = lax.rem(across + SIDE - ORDER[outer], SIDE)
            spot = inner * SIDE + outer
            copies.append(
                pltpu.make_async_copy(
                    source_ref.at[there],
                    other_ref.at[pl.ds(spot * deep, deep)],
                    sems.at[spot],
                )
            )
    for copy in copies:
        copy.start()
    for copy in copies:
        copy.wait()


def coef_kernel(place_ref, counts_ref, low_ref, high_ref, ridge_ref, scale_ref, coef_ref):
    core = place_ref[2]
    rows = scale_ref.shape[1] // 2
    position = lax.broadcasted_iota(jnp.int32, (1, 2 * rows), 1)
    other = position >= rows
    within = jnp.where(other, position - rows, position)
    used = jnp.where(other, counts_ref[1 - core], counts_ref[core])
    scale_ref[...] = jnp.where(within < used, 1.0 / used.astype(jnp.float32), 0.0)

    one = jnp.ones((1, 128), jnp.float32)
    low, high = one * low_ref[0], one * high_ref[0]
    middle, radius = (high + low) / 2.0, (high - low) / 2.0
    sigma = middle / radius
    rho = 1.0 / sigma
    rho_new = 1.0 / (2.0 * sigma - rho)
    coef_ref[0:1] = middle
    coef_ref[1:2] = one * ridge_ref[0]
    coef_ref[2:3] = rho_new * rho
    coef_ref[3:4] = 2.0 * rho_new / radius


def lay_others(place_ref, theirs, other_ref):
    deep = theirs[0].shape[1]
    _, across = line_place(place_ref)
    for inner in range(2):
        for outer in range(SIDE):
            there = lax.rem(across + SIDE - ORDER[outer], SIDE)
            at = (inner * SIDE + outer) * deep
            other_ref[at : at + deep] = theirs[inner][there]


def rhs_kernel(place_ref, coef_ref, scale_ref, parts_ref, *refs):
    mine, (own_ref, rhs_ref, inner_ref) = refs[:SIDE], refs[SIDE:]
    core = place_ref[2]
    deep, rows = mine[0].shape[1:]
    line, _ = line_place(place_ref)
    for inner in range(SIDE):
        here = lax.rem(line + SIDE - ORDER[inner], SIDE)
        for outer in range(SIDE):
            at = (inner * SIDE + outer) * deep
            own_ref[at : at + deep] = mine[outer][here]
    half = parts_ref.shape[0] // 2
    for at, side in ((core, 0), (1 - core, 1)):
        total = sum_coded(parts_ref, [2 * k + at for k in range(half)])
        rhs_ref[:, side * rows : (side + 1) * rows] = total
    first = rhs_ref[:, :rows] / coef_ref[0:1, 0:1] * scale_ref[:, :rows]
    inner_ref[...] = times(first, own_ref[...], NT)


def first_kernel(place_ref, coef_ref, scale_ref, rhs_ref, inner_ref, own_ref, first_ref, *refs):
    theirs, (second_ref, out_ref) = refs[:2], refs[2:]
    lay_others(place_ref, theirs, second_ref)
    rows = own_ref.shape[1]
    feats = (own_ref, first_ref, second_ref)
    value = rhs_ref[:, rows:] / coef_ref[0:1, 0:1] * scale_ref[:, rows:]
    from_features(inner_ref[...] + others_to_features(value, feats), feats, out_ref)


def others_to_features(value, feats):
    return jnp.concatenate([times(value, f[...], NT) for f in feats[1:]], axis=1)


def to_features(value, feats):
    rows = feats[0].shape[1]
    own = times(value[:, :rows], feats[0][...], NT)
    return own + others_to_features(value[:, rows:], feats)


def from_features(inner, feats, out_ref):
    own, first, second = (f[...] for f in feats)
    half = first.shape[0]
    left = times(inner, own, NN)
    right = times(inner[:, :half], first, NN) + times(inner[:, half:], second, NN)
    send_all(jnp.concatenate([left, right], axis=1), out_ref)


def ahead(direction, scale_ref, feats, out_ref):
    from_features(to_features(direction * scale_ref[...], feats), feats, out_ref)


def step_kernel(coef_ref, scale_ref, parts_ref, *refs):
    feats, (rhs_ref, out_ref, dir_ref, res_ref) = refs[:3], refs[3:]
    first = rhs_ref[...] / coef_ref[0:1, 0:1]
    image = sum_coded(parts_ref, range(parts_ref.shape[0])) + coef_ref[1:2, 0:1] * first
    residual = rhs_ref[...] - image
    direction = coef_ref[2:3, 0:1] * first + coef_ref[3:4, 0:1] * residual
    dir_ref[...] = direction
    res_ref[...] = residual
    ahead(direction, scale_ref, feats, out_ref)


def last_kernel(place_ref, coef_ref, scale_ref, parts_ref, *refs):
    feats, (rhs_ref, dir_ref, res_ref, out_ref, held) = refs[:3], refs[3:]
    direction = dir_ref[...]
    image = sum_coded(parts_ref, range(parts_ref.shape[0])) + coef_ref[1:2, 0:1] * direction
    residual = res_ref[...] - image
    merged = rhs_ref[...] / coef_ref[0:1, 0:1] + direction
    both = jnp.concatenate([merged, residual], axis=0) * scale_ref[...]
    held[...] = to_features(both, feats)
    width = out_ref.shape[2]
    for inner in range(SIDE):
        for outer in range(SIDE):
            at = (inner * SIDE + outer) * 2 * width
            origin = source(place_ref, ORDER[inner], ORDER[outer])
            for k in range(2):
                out_ref[origin + k] = held[:, at + k * width : at + (k + 1) * width]


def turn_kernel(blocks_ref, merged_ref, residual_ref):
    members, both, width = blocks_ref.shape
    cols = both // 2
    merged_ref[...] = blocks_ref[:, :cols].reshape(members * cols, width).T
    residual_ref[...] = blocks_ref[:, cols:].reshape(members * cols, width).T


def call(kernel, outs, specs, scratch=()):
    return pl.pallas_call(
        kernel,
        out_shape=outs,
        in_specs=specs,
        out_specs=jax.tree.map(lambda _: VMEM, outs),
        scratch_shapes=list(scratch),
        compiler_params=pltpu.CompilerParams(vmem_limit_bytes=32 * 1024 * 1024),
    )


def sum_parts(copies):
    return lax.all_to_all(copies, "z", 0, 0, tiled=True)


def body(x_first, x_second, w_first, w_second, counts, damping, eig_low, eig_high):
    f32 = jnp.float32
    shape = jax.ShapeDtypeStruct
    rows, width = x_first.shape
    members = lax.axis_size(MEMBERS)
    depth = lax.axis_size("z")
    cols = w_first.shape[1] // members
    core = lax.axis_index("core")
    place = jnp.stack([lax.axis_index("xh") * 2 + lax.axis_index("xl"), lax.axis_index("y"), core])
    place = place.astype(jnp.int32)

    lead = core == 0
    first = jnp.concatenate([x_first.T, w_first], axis=1)
    second = jnp.concatenate([x_second.T, w_second], axis=1)
    give = jnp.where(lead, second, first)
    give, *own_args = lax.optimization_barrier((give, x_first, x_second, w_first, w_second))
    kept = jnp.where(
        lead,
        jnp.concatenate([own_args[0].T, own_args[2]], axis=1),
        jnp.concatenate([own_args[1].T, own_args[3]], axis=1),
    )
    got_all = swap(give)
    mine, got = kept[:, :rows], got_all[:, :rows]
    block = jnp.where(
        lead, jnp.concatenate([mine, got], axis=0), jnp.concatenate([got, mine], axis=0)
    )
    packed = call(
        pack_kernel,
        shape((SIDE, block.shape[0] + 2 * cols, rows), jnp.bfloat16),
        [SMEM] + [VMEM] * 3,
        [pltpu.VMEM((2, members // 2, 2 * cols, width), f32), pltpu.VMEM((2 * cols, rows), f32)],
    )(place, block, kept, got_all)
    packed = exchange(packed, True)
    near = packed[:, : block.shape[0]]
    back, front = along(near, 1), along(near, 3)
    shares = call(
        line_kernel,
        shape((SIDE, 2 * cols, rows + TILE), jnp.int16),
        [VMEM] * 2,
        [pltpu.VMEM((SIDE * 2 * cols, SIDE * block.shape[0]), f32)],
    )(packed, near)
    shares, eig_low, eig_high, damping = lax.optimization_barrier(
        (shares, eig_low, eig_high, damping)
    )
    scale, coef = call(
        coef_kernel, (shape((1, 2 * rows), f32), shape((4, 128), f32)), [SMEM] * 5
    )(place, counts, eig_low, eig_high, damping)
    shares = exchange(shares, False)
    anywhere = pl.BlockSpec(memory_space=pl.ANY)
    parts, back = pl.pallas_call(
        plane_kernel,
        out_shape=(
            shape((2 * depth, cols, rows + TILE), jnp.int16),
            shape(back.shape, back.dtype),
        ),
        in_specs=[VMEM, anywhere, anywhere],
        out_specs=(VMEM, anywhere),
        input_output_aliases={1: 1},
        compiler_params=pltpu.CompilerParams(vmem_limit_bytes=32 * 1024 * 1024),
    )(shares, back, coef)
    far = along(back, 1)
    parts = lax.all_to_all(parts, ("z", "core"), 0, 0, tiled=True)
    total = members * width
    near_swapped, back_swapped = swap(near), swap(back)
    first = pl.pallas_call(
        lay_kernel,
        out_shape=shape((total // 2, rows), jnp.bfloat16),
        in_specs=[SMEM, anywhere, anywhere],
        out_specs=VMEM,
        scratch_shapes=[pltpu.SemaphoreType.DMA((2 * SIDE,))],
    )(place, near_swapped, back_swapped)
    parts, far, scale, coef, first = lax.optimization_barrier((parts, far, scale, coef, first))
    others = swap(front), swap(far)
    copies = shape((depth, cols, 2 * rows + TILE), jnp.int16)
    state = shape((cols, 2 * rows), f32)
    own, rhs, inner = call(
        rhs_kernel,
        (shape((total, rows), jnp.bfloat16), state, shape((cols, total), f32)),
        [SMEM] + [VMEM] * 7,
    )(place, coef, scale, parts, near, back, front, far)
    second, parts = call(
        first_kernel,
        (shape((total // 2, rows), jnp.bfloat16), copies),
        [SMEM] + [VMEM] * 8,
    )(place, coef, scale, rhs, inner, own, first, *others)
    feats = (own, first, second)
    parts = sum_parts(parts)
    parts, direction, residual = call(step_kernel, (copies, state, state), [VMEM] * 7)(
        coef, scale, parts, *feats, rhs
    )
    parts = sum_parts(parts)
    out = call(
        last_kernel,
        shape((members, 2 * cols, width), f32),
        [SMEM] + [VMEM] * 9,
        [pltpu.VMEM((2 * cols, total), f32)],
    )(place, coef, scale, parts, *feats, rhs, direction, residual)
    out = lax.all_to_all(out, MEMBERS, 0, 0, tiled=True)
    turned = shape((width, members * cols), f32)
    return tuple(call(turn_kernel, (turned, turned), [VMEM])(out))


def solution(mesh):
    fine = Mesh(mesh.devices.reshape(2, 8, SIDE, 2, 2), AXES)
    return jax.shard_map(
        body,
        mesh=fine,
        in_specs=(
            P(None, AXES),
            P(None, AXES),
            P(AXES, None),
            P(AXES, None),
            P(),
            P(),
            P(),
            P(),
        ),
        out_specs=(P(AXES, None), P(AXES, None)),
        check_vma=False,
    )
```

```python
import jax
import jax.numpy as jnp
from jax import lax
from jax.experimental import pallas as pl
from jax.experimental.pallas import tpu as pltpu
from jax.sharding import Mesh
from jax.sharding import PartitionSpec as P

AXES = ("xl", "z", "y", "xh", "core")
MEMBERS = ("xl", "y", "xh", "core")
SIDE = 4
ORDER = (0, 1, 3, 2)
TILE = 128
STEPS = 256.0
LARGEST = 32767.0
SMALLEST = 2.0**-125
NT = (((1,), (1,)), ((), ()))
NN = (((1,), (0,)), ((), ()))
VMEM = pl.BlockSpec(memory_space=pltpu.VMEM)
SMEM = pl.BlockSpec(memory_space=pltpu.SMEM)


def member(x, y, core):
    return (((x % 2) * SIDE + y) * 2 + x // 2) * 2 + core


def ring_pairs(shift):
    pairs = []
    for x in range(SIDE):
        for y in range(SIDE):
            for core in range(2):
                if core == 0:
                    to = member((x + shift) % SIDE, y, core)
                else:
                    to = member(x, (y + shift) % SIDE, core)
                pairs.append((member(x, y, core), to))
    return pairs


def lines(first):
    groups = []
    for core in range(2):
        for other in range(SIDE):
            spots = [(k, other) if (core == 0) != first else (other, k) for k in range(SIDE)]
            groups.append([member(x, y, core) for x, y in spots])
    return groups


def exchange(blocks, first):
    return lax.all_to_all(blocks, MEMBERS, 0, 0, axis_index_groups=lines(first), tiled=True)


def along(value, shift):
    return lax.ppermute(value, MEMBERS, ring_pairs(shift))


def swap(value):
    return lax.ppermute(value, "core", [(0, 1), (1, 0)])


def split_two(value):
    head = value.astype(jnp.bfloat16)
    tail = (value - head.astype(jnp.float32)).astype(jnp.bfloat16)
    return jnp.concatenate([head, tail], axis=0)


def times(value, feats, dims):
    out = lax.dot_general(split_two(value), feats, dims, preferred_element_type=jnp.float32)
    half = out.shape[0] // 2
    return out[:half] + out[half:]


def code(value):
    rows, lanes = value.shape
    spot = lax.broadcasted_iota(jnp.int32, (rows, TILE), 1)
    notes = jnp.zeros((rows, TILE), jnp.float32)
    pieces = []
    for t in range(lanes // TILE):
        tile = value[:, t * TILE : (t + 1) * TILE]
        peak = jnp.maximum(jnp.max(jnp.abs(tile), axis=1, keepdims=True), SMALLEST)
        note = jnp.ceil(jnp.log2(peak) * STEPS) + 1.0
        pieces.append(jnp.round(tile * jnp.exp2(note * (-1.0 / STEPS)) * LARGEST))
        notes = jnp.where(spot == t, note, notes)
    return jnp.concatenate(pieces + [notes], axis=1).astype(jnp.int32).astype(jnp.int16)


def sum_coded(parts_ref, places):
    tiles = parts_ref.shape[2] // TILE - 1
    totals = [0.0] * tiles
    for place in places:
        part = parts_ref[place].astype(jnp.int32).astype(jnp.float32)
        scales = jnp.exp2(part[:, tiles * TILE :] * (1.0 / STEPS))
        for t in range(tiles):
            totals[t] = totals[t] + part[:, t * TILE : (t + 1) * TILE] * scales[:, t : t + 1]
    return jnp.concatenate(totals, axis=1) * (1.0 / LARGEST)


def send_all(partial, out_ref):
    coded = code(partial)
    for k in range(out_ref.shape[0]):
        out_ref[k] = coded


def source(place_ref, first, second):
    x, y, core = place_ref[0], place_ref[1], place_ref[2]
    back_x = jnp.where(core == 0, second, first)
    back_y = jnp.where(core == 0, first, second)
    at_x = lax.rem(x + SIDE - back_x, SIDE)
    at_y = lax.rem(y + SIDE - back_y, SIDE)
    return ((lax.rem(at_x, 2) * SIDE + at_y) * 2 + lax.div(at_x, 2)) * 2


def line_place(place_ref):
    x, y, lead = place_ref[0], place_ref[1], place_ref[2] == 0
    return jnp.where(lead, y, x), jnp.where(lead, x, y)


def pack_kernel(place_ref, block_ref, keep_ref, got_ref, out_ref, held, strip):
    lead = place_ref[2] == 0
    deep = block_ref.shape[0]
    keep = keep_ref[:, block_ref.shape[1] :].astype(jnp.float32)
    got = got_ref[:, block_ref.shape[1] :].astype(jnp.float32)
    chips, each, width = held.shape[1:]
    for k, rows in enumerate((jnp.where(lead, keep, got), jnp.where(lead, got, keep))):
        turned = rows.T
        for chip in range(chips):
            held[k, chip] = turned[chip * each : (chip + 1) * each]
    strip[...] = jnp.zeros_like(strip)
    for at in range(SIDE):
        out_ref[at, :deep] = block_ref[...]
        for across in range(SIDE):
            x, y = jnp.where(lead, across, at), jnp.where(lead, at, across)
            chip = (lax.rem(x, 2) * SIDE + y) * 2 + lax.div(x, 2)
            for core in range(2):
                here = (2 * across + core) * width
                strip[:, here : here + width] = held[core, chip]
        out_ref[at, deep:] = strip[...].astype(out_ref.dtype)


def line_kernel(packed_ref, near_ref, out_ref, held):
    places, deep, rows = near_ref.shape
    each = out_ref.shape[1]
    for at in range(places):
        strip = packed_ref[at, deep:].astype(jnp.float32)
        for across in range(SIDE):
            part = strip[:, across * deep : (across + 1) * deep]
            held[across * each : (across + 1) * each, at * deep : (at + 1) * deep] = part
    out = lax.dot_general(
        held[...].astype(jnp.bfloat16),
        near_ref[...].reshape(places * deep, rows),
        NN,
        preferred_element_type=jnp.float32,
    )
    for across in range(SIDE):
        out_ref[across] = out[across * each : (across + 1) * each]


def plane_kernel(shares_ref, _, __, out_ref, *unused):
    total = jnp.sum(shares_ref[...], axis=0)
    cols = out_ref.shape[1]
    coded = [code(total[k * cols : (k + 1) * cols]) for k in range(2)]
    for k in range(out_ref.shape[0]):
        out_ref[k] = coded[k % 2]


def lay_kernel(place_ref, near_ref, back_ref, other_ref, sems):
    deep = near_ref.shape[1]
    _, across = line_place(place_ref)
    copies = []
    for inner, source_ref in enumerate((near_ref, back_ref)):
        for outer in range(SIDE):
            there = lax.rem(across + SIDE - ORDER[outer], SIDE)
            spot = inner * SIDE + outer
            copies.append(
                pltpu.make_async_copy(
                    source_ref.at[there],
                    other_ref.at[pl.ds(spot * deep, deep)],
                    sems.at[spot],
                )
            )
    for copy in copies:
        copy.start()
    for copy in copies:
        copy.wait()


def coef_kernel(place_ref, counts_ref, low_ref, high_ref, ridge_ref, scale_ref, coef_ref):
    core = place_ref[2]
    rows = scale_ref.shape[1] // 2
    position = lax.broadcasted_iota(jnp.int32, (1, 2 * rows), 1)
    other = position >= rows
    within = jnp.where(other, position - rows, position)
    used = jnp.where(other, counts_ref[1 - core], counts_ref[core])
    scale_ref[...] = jnp.where(within < used, 1.0 / used.astype(jnp.float32), 0.0)

    one = jnp.ones((1, 128), jnp.float32)
    low, high = one * low_ref[0], one * high_ref[0]
    middle, radius = (high + low) / 2.0, (high - low) / 2.0
    sigma = middle / radius
    rho = 1.0 / sigma
    rho_new = 1.0 / (2.0 * sigma - rho)
    coef_ref[0:1] = middle
    coef_ref[1:2] = one * ridge_ref[0]
    coef_ref[2:3] = rho_new * rho
    coef_ref[3:4] = 2.0 * rho_new / radius


def lay_others(place_ref, theirs, other_ref):
    deep = theirs[0].shape[1]
    _, across = line_place(place_ref)
    for inner in range(2):
        for outer in range(SIDE):
            there = lax.rem(across + SIDE - ORDER[outer], SIDE)
            at = (inner * SIDE + outer) * deep
            other_ref[at : at + deep] = theirs[inner][there]


def rhs_kernel(place_ref, coef_ref, scale_ref, parts_ref, *refs):
    mine, (own_ref, rhs_ref, inner_ref) = refs[:SIDE], refs[SIDE:]
    core = place_ref[2]
    deep, rows = mine[0].shape[1:]
    line, _ = line_place(place_ref)
    for inner in range(SIDE):
        here = lax.rem(line + SIDE - ORDER[inner], SIDE)
        for outer in range(SIDE):
            at = (inner * SIDE + outer) * deep
            own_ref[at : at + deep] = mine[outer][here]
    half = parts_ref.shape[0] // 2
    for at, side in ((core, 0), (1 - core, 1)):
        total = sum_coded(parts_ref, [2 * k + at for k in range(half)])
        rhs_ref[:, side * rows : (side + 1) * rows] = total
    first = rhs_ref[:, :rows] / coef_ref[0:1, 0:1] * scale_ref[:, :rows]
    inner_ref[...] = times(first, own_ref[...], NT)


def first_kernel(place_ref, coef_ref, scale_ref, rhs_ref, inner_ref, own_ref, first_ref, *refs):
    theirs, (second_ref, out_ref) = refs[:2], refs[2:]
    lay_others(place_ref, theirs, second_ref)
    rows = own_ref.shape[1]
    feats = (own_ref, first_ref, second_ref)
    value = rhs_ref[:, rows:] / coef_ref[0:1, 0:1] * scale_ref[:, rows:]
    from_features(inner_ref[...] + others_to_features(value, feats), feats, out_ref)


def others_to_features(value, feats):
    return jnp.concatenate([times(value, f[...], NT) for f in feats[1:]], axis=1)


def to_features(value, feats):
    rows = feats[0].shape[1]
    own = times(value[:, :rows], feats[0][...], NT)
    return own + others_to_features(value[:, rows:], feats)


def from_features(inner, feats, out_ref):
    own, first, second = (f[...] for f in feats)
    half = first.shape[0]
    left = times(inner, own, NN)
    right = times(inner[:, :half], first, NN) + times(inner[:, half:], second, NN)
    send_all(jnp.concatenate([left, right], axis=1), out_ref)


def ahead(direction, scale_ref, feats, out_ref):
    from_features(to_features(direction * scale_ref[...], feats), feats, out_ref)


def step_kernel(coef_ref, scale_ref, parts_ref, *refs):
    feats, (rhs_ref, out_ref, dir_ref, res_ref) = refs[:3], refs[3:]
    first = rhs_ref[...] / coef_ref[0:1, 0:1]
    image = sum_coded(parts_ref, range(parts_ref.shape[0])) + coef_ref[1:2, 0:1] * first
    residual = rhs_ref[...] - image
    direction = coef_ref[2:3, 0:1] * first + coef_ref[3:4, 0:1] * residual
    dir_ref[...] = direction
    res_ref[...] = residual
    ahead(direction, scale_ref, feats, out_ref)


def last_kernel(place_ref, coef_ref, scale_ref, parts_ref, *refs):
    feats, (rhs_ref, dir_ref, res_ref, out_ref, held) = refs[:3], refs[3:]
    direction = dir_ref[...]
    image = sum_coded(parts_ref, range(parts_ref.shape[0])) + coef_ref[1:2, 0:1] * direction
    residual = res_ref[...] - image
    merged = rhs_ref[...] / coef_ref[0:1, 0:1] + direction
    both = jnp.concatenate([merged, residual], axis=0) * scale_ref[...]
    held[...] = to_features(both, feats)
    width = out_ref.shape[2]
    for inner in range(SIDE):
        for outer in range(SIDE):
            at = (inner * SIDE + outer) * 2 * width
            origin = source(place_ref, ORDER[inner], ORDER[outer])
            for k in range(2):
                out_ref[origin + k] = held[:, at + k * width : at + (k + 1) * width]


def turn_kernel(blocks_ref, merged_ref, residual_ref):
    members, both, width = blocks_ref.shape
    cols = both // 2
    merged_ref[...] = blocks_ref[:, :cols].reshape(members * cols, width).T
    residual_ref[...] = blocks_ref[:, cols:].reshape(members * cols, width).T


def call(kernel, outs, specs, scratch=()):
    return pl.pallas_call(
        kernel,
        out_shape=outs,
        in_specs=specs,
        out_specs=jax.tree.map(lambda _: VMEM, outs),
        scratch_shapes=list(scratch),
        compiler_params=pltpu.CompilerParams(vmem_limit_bytes=32 * 1024 * 1024),
    )


def sum_parts(copies):
    return lax.all_to_all(copies, "z", 0, 0, tiled=True)


def body(x_first, x_second, w_first, w_second, counts, damping, eig_low, eig_high):
    f32 = jnp.float32
    shape = jax.ShapeDtypeStruct
    rows, width = x_first.shape
    members = lax.axis_size(MEMBERS)
    depth = lax.axis_size("z")
    cols = w_first.shape[1] // members
    core = lax.axis_index("core")
    place = jnp.stack([lax.axis_index("xh") * 2 + lax.axis_index("xl"), lax.axis_index("y"), core])
    place = place.astype(jnp.int32)

    lead = core == 0
    first = jnp.concatenate([x_first.T, w_first], axis=1)
    second = jnp.concatenate([x_second.T, w_second], axis=1)
    kept, give = jnp.where(lead, first, second), jnp.where(lead, second, first)
    got_all = swap(give)
    mine, got = kept[:, :rows], got_all[:, :rows]
    block = jnp.where(
        lead, jnp.concatenate([mine, got], axis=0), jnp.concatenate([got, mine], axis=0)
    )
    packed = call(
        pack_kernel,
        shape((SIDE, block.shape[0] + 2 * cols, rows), jnp.bfloat16),
        [SMEM] + [VMEM] * 3,
        [pltpu.VMEM((2, members // 2, 2 * cols, width), f32), pltpu.VMEM((2 * cols, rows), f32)],
    )(place, block, kept, got_all)
    packed = exchange(packed, True)
    near = packed[:, : block.shape[0]]
    back, front = along(near, 1), along(near, 3)
    shares = call(
        line_kernel,
        shape((SIDE, 2 * cols, rows), f32),
        [VMEM] * 2,
        [pltpu.VMEM((SIDE * 2 * cols, SIDE * block.shape[0]), f32)],
    )(packed, near)
    shares, eig_low, eig_high, damping = lax.optimization_barrier(
        (shares, eig_low, eig_high, damping)
    )
    scale, coef = call(
        coef_kernel, (shape((1, 2 * rows), f32), shape((4, 128), f32)), [SMEM] * 5
    )(place, counts, eig_low, eig_high, damping)
    shares = exchange(shares, False)
    anywhere = pl.BlockSpec(memory_space=pl.ANY)
    parts, back = pl.pallas_call(
        plane_kernel,
        out_shape=(
            shape((2 * depth, cols, rows + TILE), jnp.int16),
            shape(back.shape, back.dtype),
        ),
        in_specs=[VMEM, anywhere, anywhere],
        out_specs=(VMEM, anywhere),
        input_output_aliases={1: 1},
        compiler_params=pltpu.CompilerParams(vmem_limit_bytes=32 * 1024 * 1024),
    )(shares, back, coef)
    far = along(back, 1)
    parts = lax.all_to_all(parts, ("z", "core"), 0, 0, tiled=True)
    total = members * width
    near_swapped, back_swapped = swap(near), swap(back)
    first = pl.pallas_call(
        lay_kernel,
        out_shape=shape((total // 2, rows), jnp.bfloat16),
        in_specs=[SMEM, anywhere, anywhere],
        out_specs=VMEM,
        scratch_shapes=[pltpu.SemaphoreType.DMA((2 * SIDE,))],
    )(place, near_swapped, back_swapped)
    parts, far, scale, coef, first = lax.optimization_barrier((parts, far, scale, coef, first))
    others = swap(front), swap(far)
    copies = shape((depth, cols, 2 * rows + TILE), jnp.int16)
    state = shape((cols, 2 * rows), f32)
    own, rhs, inner = call(
        rhs_kernel,
        (shape((total, rows), jnp.bfloat16), state, shape((cols, total), f32)),
        [SMEM] + [VMEM] * 7,
    )(place, coef, scale, parts, near, back, front, far)
    second, parts = call(
        first_kernel,
        (shape((total // 2, rows), jnp.bfloat16), copies),
        [SMEM] + [VMEM] * 8,
    )(place, coef, scale, rhs, inner, own, first, *others)
    feats = (own, first, second)
    parts = sum_parts(parts)
    parts, direction, residual = call(step_kernel, (copies, state, state), [VMEM] * 7)(
        coef, scale, parts, *feats, rhs
    )
    parts = sum_parts(parts)
    out = call(
        last_kernel,
        shape((members, 2 * cols, width), f32),
        [SMEM] + [VMEM] * 9,
        [pltpu.VMEM((2 * cols, total), f32)],
    )(place, coef, scale, parts, *feats, rhs, direction, residual)
    out = lax.all_to_all(out, MEMBERS, 0, 0, tiled=True)
    turned = shape((width, members * cols), f32)
    return tuple(call(turn_kernel, (turned, turned), [VMEM])(out))


def solution(mesh):
    fine = Mesh(mesh.devices.reshape(2, 8, SIDE, 2, 2), AXES)
    return jax.shard_map(
        body,
        mesh=fine,
        in_specs=(
            P(None, AXES),
            P(None, AXES),
            P(AXES, None),
            P(AXES, None),
            P(),
            P(),
            P(),
            P(),
        ),
        out_specs=(P(AXES, None), P(AXES, None)),
        check_vma=False,
    )
```
